256 devices in a mesh: grp: 16 (over y, x), tp: 16 (over z, core).
Axes of the slice: x: 4, y: 4, z: 8, core: 2. Of those that a mesh axis runs over, the one named last changes fastest.
Arguments:
- hidden: bfloat16 [294912, 5120], P(('grp', 'tp')), may hold values from -6 to 6
- lengths: int32 [16, 16], P('grp'), may hold values from 1 to 1152, 7372 in all within a row
- kv_weight: bfloat16 [5120, 1024], P('grp', 'tp'), may hold values from -0.078125 to 0.078125
- input_gain: float32 [5120], replicated, may hold values from 0.1 to 1.9
- key_gain: float32 [128], replicated, may hold values from 0.1 to 1.9
Outputs:
- cache_pages: bfloat16 [1280, 128, 1024], P(('grp', 'tp'))
The draws below stay inside these ranges and needn't reach their ends.
Inputs may be any that keep to these rules, and one draw needn't show every extreme that they name: In each group's row the 16 lengths sum to 7372 and the largest equals 1152.
All inputs are finite; a program needn't handle non-finite values.
Results may differ from the reference program's by a relative error of at most 0.0049.
Values may be sent and summed in bfloat16 or wider, within the bound.
A program may use at most 64 MiB of HBM per device.

```python
import math
import jax
import jax.numpy as jnp
import numpy as np
from jax import lax

D = 5120
HD = 128
KVH = 4
BLK = 128
B_IN = 9
LIVE_SUM = 7372
B_BAL = 5
TOKENS = 294912
N_GRP = 16
N_TP = 16


def block_scale(rng, dims, split, least, top_value):
    level, own = 1.0, jax.random.fold_in(rng, 6)
    for dim, parts in split:
        heights = jnp.exp(jax.random.uniform(jax.random.fold_in(own, dim), (parts,), jnp.float32, least / len(split), top_value / len(split)))
        level = level * jnp.repeat(heights, dims[dim] // parts).reshape([-1 if axis == dim else 1 for axis in range(len(dims))])
    return level


def length_profile(count, total, reach, lean):
    portions = [(1 << 20) // math.isqrt(grade ** lean) + 1 for grade in range(2, count + 1)]
    rest, given = total - reach - (count - 1), [1] * (count - 1)
    while rest > 0:
        free = [i for i in range(count - 1) if given[i] < reach]
        whole, remaining = sum([portions[i] for i in free]), rest
        for i in free:
            extra = min(reach - given[i], max(1, remaining * portions[i] // whole), rest)
            given[i] = given[i] + extra
            rest = rest - extra
    return np.array([reach] + given)


def uneven(key, amount, total, bound, lean):
    if amount == 2:
        one = jax.random.randint(key, (), max(1, total - bound), min(bound, total - 1) + 1)
        return jnp.stack([one, total - one])
    sizes = jnp.asarray(length_profile(amount, total, bound, lean), jnp.int32)
    pairs = (amount - 1) // 2
    donor, sink = sizes[1:1 + 2 * pairs:2], sizes[2:2 + 2 * pairs:2]
    room = jnp.minimum(donor - 1, bound - sink)
    passed = jax.random.randint(jax.random.fold_in(key, 1), (pairs,), 0, 1 << 20) % (room + 1)
    sizes = sizes.at[1:1 + 2 * pairs:2].set(donor - passed).at[2:2 + 2 * pairs:2].set(sink + passed)
    return sizes[jax.random.permutation(jax.random.fold_in(key, 2), amount)]


def scatter_about(rng, shape, width, limit, split=(), kind=jnp.bfloat16):
    array = jax.random.normal(rng, shape, jnp.float32) * width
    if len(split) > 0:
        array = block_scale(rng, shape, split, -0.22, 0.18) * array
    return jnp.clip(array, min=-limit, max=limit).astype(kind)


def setup_inputs(seed: int = 0) -> dict:
    seeds = jax.random.split(jax.random.key(seed), 6)
    hidden = scatter_about(seeds[0], (TOKENS, D), 1.0, 6.0, ((0, 256),))
    lengths = jax.vmap(lambda own: uneven(own, N_TP, LIVE_SUM, B_IN * BLK, 2))(jax.random.split(seeds[1], N_GRP)).reshape((N_GRP, N_TP)).astype(jnp.int32)
    kv_weight = scatter_about(seeds[2], (D, 2 * KVH * HD), D ** -0.5, 0.078125, ((0, 16), (1, 16)))
    input_gain = jnp.clip(1.0 + 0.18 * jax.random.normal(seeds[3], (D,), jnp.float32), 0.1, 1.9)
    key_gain = jnp.clip(1.0 + 0.18 * jax.random.normal(seeds[4], (HD,), jnp.float32), 0.1, 1.9)
    return {"hidden": hidden, "lengths": lengths, "kv_weight": kv_weight, "input_gain": input_gain, "key_gain": key_gain}


rope_base = 1000000.0
norm_eps = 1e-06

def normalize(token_rows, input_gain):
    values = token_rows.astype(jnp.float32)
    row_scale = lax.rsqrt(lax.optimization_barrier(jnp.mean(values * values, axis=-1, keepdims=True)) + norm_eps)
    return (values * row_scale * input_gain).astype(jnp.bfloat16)

def finish(projected, positions, valid, key_gain):
    key_width = KVH * HD
    half_dim = HD // 2
    row_count = projected.shape[0]
    key_part = projected[:, :key_width].reshape(row_count, KVH, HD)
    key_scale = lax.rsqrt(lax.optimization_barrier(jnp.mean(key_part * key_part, axis=-1, keepdims=True)) + norm_eps)
    key_part = key_part * key_scale * key_gain
    exponent = jnp.arange(half_dim, dtype=jnp.float32) * (2.0 / HD)
    inverse = jnp.exp(exponent * -math.log(rope_base))
    angles = positions.astype(jnp.float32)[:, None] * inverse[None, :]
    cosine = jnp.cos(angles)[:, None, :]
    sine_part = jnp.sin(angles)[:, None, :]
    lower_half = key_part[..., :half_dim]
    upper_half = key_part[..., half_dim:]
    turned = jnp.concatenate([lower_half * cosine - upper_half * sine_part, upper_half * cosine + lower_half * sine_part], axis=-1)
    merged = jnp.concatenate([turned.reshape(row_count, key_width), projected[:, key_width:]], axis=-1)
    return jnp.where(valid[:, None], merged, 0.0).astype(jnp.bfloat16)

def reference(hidden, lengths, kv_weight, input_gain, key_gain):
    block_rows = hidden.reshape(N_GRP, N_TP * B_IN, BLK, D)
    block_counts = ((lengths + (BLK - 1)) // BLK).astype(jnp.int32)
    block_ends = jnp.cumsum(block_counts, axis=1).astype(jnp.int32)
    block_starts = (block_ends - block_counts).astype(jnp.int32)
    page_slots = jnp.arange(N_TP, dtype=jnp.int32)[:, None] + N_TP * jnp.arange(B_BAL, dtype=jnp.int32)[None, :]
    page_ranks = page_slots.reshape(-1)
    offsets = jnp.arange(BLK, dtype=jnp.int32)

    def one_group(group_data):
        group_blocks, group_len, group_ends, group_starts = group_data
        anchor = jnp.minimum(lax.optimization_barrier(jnp.sum((group_ends[None, :] <= page_ranks[:, None]).astype(jnp.int32), axis=1)).astype(jnp.int32), N_TP - 1)
        block_index = (page_ranks - group_starts[anchor]).astype(jnp.int32)
        page_live = page_ranks < group_ends[-1]
        flat_index = (anchor * B_IN + jnp.clip(block_index, 0, B_IN - 1)).astype(jnp.int32)
        token_rows = jnp.take(group_blocks, flat_index, axis=0).reshape(-1, D)
        positions = block_index[:, None] * BLK + offsets[None, :]
        valid = page_live[:, None] & (positions < group_len[anchor][:, None])
        projected = jnp.dot(normalize(token_rows, input_gain), kv_weight, preferred_element_type=jnp.float32)
        return finish(projected, positions.reshape(-1), valid.reshape(-1), key_gain).reshape(N_TP * B_BAL, BLK, 2 * KVH * HD)
    cache_pages = lax.map(one_group, (block_rows, lengths, block_ends, block_starts))
    return cache_pages.reshape(N_GRP * N_TP * B_BAL, BLK, 2 * KVH * HD)
```

```python
import functools
import math

import jax
import jax.numpy as jnp
import numpy as np
from jax import lax
from jax.experimental import pallas as pl
from jax.experimental.pallas import tpu as pltpu
from jax.sharding import PartitionSpec as P

HD = 128
BLK = 128
NB = 9
NZ = 8
PAGES = 5
NC = 8
EPS = 1e-06
MESH = pl.DeviceIdType.MESH
BF, F32, I32 = jnp.bfloat16, jnp.float32, jnp.int32

CA = (5, 4, 3, 2)
CB = (4, 3, 2)
SRC = 10
BASE_A = tuple(SRC + sum(CA[:i]) for i in range(4))
BASE_B = tuple(SRC + sum(CA) + sum(CB[:i]) for i in range(3))
ZERO = SRC + sum(CA) + sum(CB)
T_LEN, T_P, T_O, T_A, T_B, T_F = 0, 1, 6, 11, 16, 20
T_SIZE = 32


def tables(first, length, z, c, where):
    d = 1 - 2 * c
    seq = 2 * z + c

    def begin(zz):
        return (first(2 * zz) - c + 1) >> 1

    out = {T_LEN: length}
    fs = first(seq)
    for e in range(5):
        b = ((fs + 1 - c) & 1) + 2 * e
        out[T_P + e] = where(b > NB - 1, NB - 1, b)
        b = ((fs + c) & 1) + 2 * e
        out[T_O + e] = where(b > NB - 1, NB - 1, b)
    m0, m1 = begin(z), begin(z + 1)
    q0 = ((first(2 * z + 1) - c + 1) >> 1) - m0

    def source_index(u):
        lead = u < q0
        v = where(c == 0, where(lead, u, 5 + u - q0), where(lead, 5 + u, u - q0))
        v = where(v < 0, 0, v)
        return where(v > SRC - 1, SRC - 1, v)

    for base, slots, order in ((T_A, CA[0], (4, 3, 2, 1)), (T_B, CB[0], (5, 6, 7))):
        pos = 0
        table = [0] * slots
        for kap in order:
            first_m = m0 + ((z + d * kap - m0) & 7)
            for e in range(2):
                m = first_m + 8 * e
                present = m < m1
                value = source_index(m - m0)
                for q in range(slots):
                    table[q] = where(present & (pos == q), value, table[q])
                pos = pos + where(present, 1, 0)
        for q in range(slots):
            out[base + q] = table[q]
    total = first(2 * NZ)
    begins = [begin(i) for i in range(NZ + 1)]
    for s in range(PAGES):
        m = 8 * s + z
        zs = 0
        for i in range(NZ - 1):
            zs = zs + where(begins[i + 1] <= m, 1, 0)
        s0, s1 = begins[0], begins[1]
        for i in range(1, NZ):
            s0 = where(zs == i, begins[i], s0)
            s1 = where(zs == i, begins[i + 1], s1)
        kap = (d * (z - zs)) & 7
        second = where(m - 8 >= s0, 1, 0)

        def count(k):
            f = s0 + ((zs + d * k - s0) & 7)
            return where(f < s1, 1, 0) + where(f + 8 < s1, 1, 0)

        value = source_index(m - m0)
        pos = second
        for k in (4, 3, 2, 1):
            value = where(kap == k, BASE_A[k - 1] + pos, value)
            pos = pos + count(k)
        pos = second
        for k in (5, 6, 7):
            value = where(kap == k, BASE_B[7 - k] + pos, value)
            pos = pos + count(k)
        out[T_F + s] = where(16 * s + 2 * z + c < total, value, ZERO)
    return out


def table_kernel(len_ref, tab_ref, first_ref):
    t = lax.axis_index("tp")
    z, c = t // 2, t % 2
    running = jnp.int32(0)
    first_ref[0] = running
    for i in range(2 * NZ):
        running = running + ((len_ref[0, i] + (BLK - 1)) >> 7)
        first_ref[i + 1] = running
    out = tables(lambda i: first_ref[i], len_ref[0, t], z, c, jnp.where)
    for i in range(T_SIZE):
        tab_ref[i] = jnp.asarray(out.get(i, 0), I32)


def main_kernel(ny, nx, rows, depth, *refs):
    (tab, wp, kg, cs_hbm, x_hbm, out,
     xv, csv, rs, W, pairb, own, acc, src, fin, stp, prv, sta, stb,
     ra1, ra2, ra3, ra4, rb1, rb2, rb3,
     x_sem, cs_sem, pair_s, pair_r, z_s, z_r, p1_s, p1_r, p2_s, p2_r, h_s, h_r, a2a_s, a2a_r) = refs
    ra, rb = (ra1, ra2, ra3, ra4), (rb1, rb2, rb3)
    half = depth // (ny * nx * 2)
    g, t = lax.axis_index("grp"), lax.axis_index("tp")
    z, c = t // 2, t % 2
    y, x = g // nx, g % nx
    d = 1 - 2 * c

    def dev(gg, tt):
        return {"grp": gg, "tp": tt}

    partner = dev(g, t + d)
    z_peers = [dev(g, 2 * ((z + k) % NZ) + c) for k in range(1, NZ)]
    far = dev(g, 2 * ((z + d + NZ) % NZ) + c)
    near = dev(g, 2 * ((z - d + NZ) % NZ) + c)
    x_peers = [dev(y * nx + (x + k) % nx, t) for k in range(1, nx)]
    y_peers = [dev(((y + k) % ny) * nx + x, t) for k in range(1, ny)]

    def x_copy(b):
        rows_b = pl.ds(pl.multiple_of(b * BLK, BLK), BLK)
        return pltpu.make_async_copy(x_hbm.at[rows_b], xv.at[rows_b], x_sem.at[b])

    cs_copy = pltpu.make_async_copy(cs_hbm, csv, cs_sem)

    @pl.loop(0, NB)
    def _(b):
        x_copy(b).start()

    cs_copy.start()

    barrier = pltpu.get_barrier_semaphore()
    everyone = [partner, *z_peers, *x_peers, *y_peers]
    for p in everyone:
        pl.semaphore_signal(barrier, inc=1, device_id=p, device_id_type=MESH)
    pl.semaphore_wait(barrier, len(everyone))

    def remote(s, r, ss, rr, p):
        return pltpu.make_async_remote_copy(
            src_ref=s, dst_ref=r, send_sem=ss, recv_sem=rr, device_id=p, device_id_type=MESH
        )

    pair_copy = remote(
        wp.at[pl.ds(pl.multiple_of((1 - c) * half, half), half)], pairb, pair_s, pair_r, partner
    )
    pair_copy.start()
    pair_copy.wait_recv()
    mine = wp[pl.ds(pl.multiple_of(c * half, half), half)]
    W[z, y, x, c] = mine + pairb[...]

    def z_copy(k):
        return remote(W.at[z, y, x, c], W.at[z, y, x, c], z_s.at[k], z_r.at[z], z_peers[k])

    for k in (0, NZ - 2, 1, NZ - 3, 2, NZ - 4, 3):
        z_copy(k).start()

    def piece(n, yy, xx):
        return W.at[n, yy, xx, c]

    def at_x(k):
        return (y, (x + k) % nx)

    def at_y(k):
        return ((y + k) % ny, x)

    def pick(a, b):
        return jax.tree.map(lambda i, j: jnp.where(c == 0, i, j), a, b)

    np1, np2 = nx - 1, ny - 1
    first_peer = [pick(x_peers[k], y_peers[k]) for k in range(np1)]
    second_peer = [pick(y_peers[k], x_peers[k]) for k in range(np2)]

    def p1_copy(n, k):
        return remote(piece(n, y, x), piece(n, y, x), p1_s.at[n, k], p1_r.at[n, k], first_peer[k])

    def p2_copy(n, j, l):
        yy, xx = (y, x) if j == 0 else pick(at_x(nx - j), at_y(ny - j))
        return remote(piece(n, yy, xx), piece(n, yy, xx), p2_s.at[n, j, l], p2_r.at[n], second_peer[l])

    def phase1(n):
        @pl.when(n != z)
        def _():
            pltpu.make_async_copy(W.at[0, 0, 0, 0], W.at[0, 0, 0, 0], z_r.at[n]).wait()

        for k in range(np1):
            p1_copy(n, k).start()
        for l in range(np2):
            p2_copy(n, 0, l).start()

    def phase2(n):
        for k in range(np1):
            pltpu.make_async_copy(W.at[0, 0, 0, 0], W.at[0, 0, 0, 0], p1_r.at[n, k]).wait()
            for l in range(np2):
                p2_copy(n, k + 1, l).start()

    def hand_copy(n):
        return remote(W.at[n, :, :, c], W.at[n, :, :, c], h_s.at[n], h_r.at[n], partner)

    def hand_over(n):
        if np2:
            dummy = W.at[0, pl.ds(0, np2), :, 0]
            pltpu.make_async_copy(dummy, dummy, p2_r.at[n]).wait()
        hand_copy(n).start()

    phase1(0)
    phase1(1)
    phase1(2)
    phase2(0)
    phase2(1)

    length = tab[T_LEN]

    @pl.loop(0, NB)
    def _(b):
        x_copy(b).wait()

        @pl.loop(0, BLK // 16)
        def _(i):
            r0 = pl.multiple_of(b * BLK + i * 16, 16)
            v = xv[pl.ds(r0, 16), :].astype(F32)
            mean = jnp.sum(v * v, axis=1, keepdims=True) * (1.0 / depth)
            scale = jnp.broadcast_to(lax.rsqrt(mean + EPS), (16, HD))
            p = r0 + lax.broadcasted_iota(I32, (16, HD), 0)
            rs[pl.ds(r0, 16), :] = jnp.where(p < length, scale, 0.0)

    cs_copy.wait()
    hand_over(0)
    fin[ZERO] = jnp.zeros((BLK, HD), BF)

    def compute(n):
        tile = 3 * BLK

        @pl.loop(0, NB // 3)
        def _(i):
            r0 = pl.multiple_of(i * tile, tile)
            rows_i = pl.ds(r0, tile)
            w = W[n].reshape(depth, HD)
            a = jnp.dot(xv[rows_i, :], w, preferred_element_type=F32)
            acc[...] = a * rs[rows_i, :]

            @pl.when(n < NC // 2)
            def _():
                k = acc[...]
                s = lax.rsqrt(jnp.mean(k * k, axis=1, keepdims=True) + EPS)
                k = k * s * kg[...]
                turned = k * csv[0, rows_i, :] + pltpu.roll(k, HD // 2, 1) * csv[1, rows_i, :]
                own[pl.ds(3 * i, 3)] = turned.astype(BF).reshape(3, BLK, HD)

            @pl.when(n >= NC // 2)
            def _():
                own[pl.ds(3 * i, 3)] = acc[...].astype(BF).reshape(3, BLK, HD)

    def pair_block_copy(n):
        return remote(stp.at[n], prv.at[n], a2a_s.at[n, 0], a2a_r.at[n, 0], partner)

    def hop_a(n, h):
        s = sta.at[n] if h == 0 else ra[h - 1].at[n, pl.ds(0, CA[h])]
        return remote(s, ra[h].at[n], a2a_s.at[n, 1 + h], a2a_r.at[n, 1 + h], far)

    def hop_b(n, h):
        s = stb.at[n] if h == 0 else rb[h - 1].at[n, pl.ds(0, CB[h])]
        return remote(s, rb[h].at[n], a2a_s.at[n, 5 + h], a2a_r.at[n, 5 + h], near)

    def send_first(n):
        for e in range(5):
            stp[n, e] = own[tab[T_P + e]]
        pair_block_copy(n).start()
        for e in range(5):
            src[n, e] = own[tab[T_O + e]]
        pair_block_copy(n).wait_recv()
        for e in range(5):
            src[n, 5 + e] = prv[n, e]
            fin[e] = src[n, e]
            fin[5 + e] = prv[n, e]
        for q in range(CA[0]):
            sta[n, q] = fin[tab[T_A + q]]
        for q in range(CB[0]):
            stb[n, q] = fin[tab[T_B + q]]
        hop_a(n, 0).start()
        hop_b(n, 0).start()

    def forward(n, h):
        hop_a(n, h - 1).wait_recv()
        if h < 4:
            hop_a(n, h).start()
        if h - 1 < 3:
            hop_b(n, h - 1).wait_recv()
        if h < 3:
            hop_b(n, h).start()

    def assemble(n):
        for e in range(SRC):
            fin[e] = src[n, e]
        for h in range(4):
            for q in range(CA[h]):
                fin[BASE_A[h] + q] = ra[h][n, q]
        for h in range(3):
            for q in range(CB[h]):
                fin[BASE_B[h] + q] = rb[h][n, q]
        columns = pl.ds(pl.multiple_of(n * HD, HD), HD)
        for s in range(PAGES):
            out[s, :, columns] = fin[tab[T_F + s]]

    @pl.loop(0, NC + 4)
    def _(n):
        @pl.when(n < NC)
        def _():
            hand_copy(n).wait_recv()

            @pl.when(n + 3 < NC)
            def _():
                phase1(n + 3)

            @pl.when(n + 2 < NC)
            def _():
                phase2(n + 2)

            compute(n)

            @pl.when(n + 1 < NC)
            def _():
                hand_over(n + 1)

            send_first(n)

        for h in (1, 2, 3, 4):
            @pl.when((n - h >= 0) & (n - h < NC))
            def _():
                forward(n - h, h)
                if h == 4:
                    assemble(n - h)

    pair_copy.wait_send()
    for k in range(NZ - 1):
        z_copy(k).wait_send()

    @pl.loop(0, NC)
    def _(n):
        for k in range(np1):
            p1_copy(n, k).wait_send()
        for j in range(np1 + 1):
            for l in range(np2):
                p2_copy(n, j, l).wait_send()
        hand_copy(n).wait_send()
        pair_block_copy(n).wait_send()
        for h in range(4):
            hop_a(n, h).wait_send()
        for h in range(3):
            hop_b(n, h).wait_send()


def rotary(rows):
    m = np.arange(HD // 2, dtype=np.float64)
    angle = np.arange(rows, dtype=np.float64)[:, None] * (1000000.0 ** (-2.0 * m / HD))[None, :]
    cos, sin = np.cos(angle), np.sin(angle)
    return np.stack([np.concatenate([cos, cos], 1), np.concatenate([-sin, sin], 1)]).astype(np.float32)


def local(ny, nx, hidden, lengths, kv_weight, input_gain, key_gain):
    rows, depth = hidden.shape
    piece = depth // (ny * nx)
    g, t = lax.axis_index("grp"), lax.axis_index("tp")
    vm, sm, anym = (pl.BlockSpec(memory_space=s) for s in (pltpu.VMEM, pltpu.SMEM, pl.ANY))
    tab = pl.pallas_call(
        table_kernel,
        out_shape=jax.ShapeDtypeStruct((T_SIZE,), I32),
        in_specs=[sm],
        out_specs=sm,
        scratch_shapes=[pltpu.SMEM((2 * NZ + 1,), I32)],
        name="tables",
    )(lengths)
    gain = lax.dynamic_slice(input_gain, (g * piece,), (piece,))
    scaled = (kv_weight.astype(F32) * gain[:, None]).astype(BF)
    lane = lax.broadcasted_iota(I32, (piece, HD), 1) // (HD // 2)
    wp = jnp.where(lane == t % 2, jnp.concatenate([scaled, scaled], axis=1), jnp.zeros((), BF))
    blk = lambda *s: pltpu.VMEM((*s, BLK, HD), BF)
    dma = lambda *s: pltpu.SemaphoreType.DMA(s)
    half = piece // 2
    return pl.pallas_call(
        functools.partial(main_kernel, ny, nx, rows, depth),
        out_shape=jax.ShapeDtypeStruct((PAGES, BLK, NC * HD), BF),
        in_specs=[sm, vm, vm, anym, anym],
        out_specs=vm,
        scratch_shapes=[
            pltpu.VMEM((rows, depth), BF),
            pltpu.VMEM((2, rows, HD), F32),
            pltpu.VMEM((rows, HD), F32),
            pltpu.VMEM((NC, ny, nx, 2, half, HD), BF),
            pltpu.VMEM((half, HD), BF),
            blk(NB),
            pltpu.VMEM((3 * BLK, HD), F32),
            blk(NC, SRC),
            blk(ZERO + 1),
            blk(NC, 5),
            blk(NC, 5),
            blk(NC, CA[0]),
            blk(NC, CB[0]),
            *[blk(NC, s) for s in CA],
            *[blk(NC, s) for s in CB],
            dma(NB),
            pltpu.SemaphoreType.DMA,
            pltpu.SemaphoreType.DMA,
            pltpu.SemaphoreType.DMA,
            dma(NZ - 1),
            dma(NC),
            dma(NC, max(nx - 1, 1)),
            dma(NC, max(nx - 1, 1)),
            dma(NC, nx, max(ny - 1, 1)),
            dma(NC),
            dma(NC),
            dma(NC),
            dma(NC, 8),
            dma(NC, 8),
        ],
        compiler_params=pltpu.CompilerParams(
            collective_id=0, has_side_effects=True, vmem_limit_bytes=66_000_000
        ),
        name="recompute",
    )(tab, wp, key_gain[None, :], jnp.asarray(rotary(rows)), hidden)


def solution(mesh):
    side = math.isqrt(mesh.shape["grp"])
    placed = (P(("grp", "tp"), None), P("grp", None), P("grp", "tp"), P(), P())
    return jax.shard_map(
        functools.partial(local, side, side),
        mesh=mesh,
        in_specs=placed,
        out_specs=P(("grp", "tp"), None, None),
        check_vma=False,
    )
```

```python
import functools
import math

import jax
import jax.numpy as jnp
import numpy as np
from jax import lax
from jax.experimental import pallas as pl
from jax.experimental.pallas import tpu as pltpu
from jax.sharding import PartitionSpec as P

HD = 128
BLK = 128
NB = 9
NZ = 8
PAGES = 5
NC = 4
CW = 256
EPS = 1e-06
MESH = pl.DeviceIdType.MESH
BF, F32, I32 = jnp.bfloat16, jnp.float32, jnp.int32

CA = (5, 4, 3, 2)
CB = (4, 3, 2)
SRC = 10
BASE_A = tuple(SRC + sum(CA[:i]) for i in range(4))
BASE_B = tuple(SRC + sum(CA) + sum(CB[:i]) for i in range(3))
ZERO = SRC + sum(CA) + sum(CB)
NS = ZERO + 1
T_LEN, T_P, T_O, T_A, T_B, T_F, T_J = 0, 1, 6, 11, 16, 20, 25
T_SIZE = 32


def tables(first, length, z, c, where):
    d = 1 - 2 * c
    seq = 2 * z + c

    def begin(zz):
        return (first(2 * zz) - c + 1) >> 1

    out = {T_LEN: length}
    fs = first(seq)
    for e in range(5):
        b = ((fs + 1 - c) & 1) + 2 * e
        out[T_P + e] = where(b > NB - 1, NB - 1, b)
        b = ((fs + c) & 1) + 2 * e
        out[T_O + e] = where(b > NB - 1, NB - 1, b)
    m0, m1 = begin(z), begin(z + 1)
    q0 = ((first(2 * z + 1) - c + 1) >> 1) - m0

    def source_index(u):
        lead = u < q0
        v = where(c == 0, where(lead, u, 5 + u - q0), where(lead, 5 + u, u - q0))
        v = where(v < 0, 0, v)
        return where(v > SRC - 1, SRC - 1, v)

    for base, slots, order in ((T_A, CA[0], (4, 3, 2, 1)), (T_B, CB[0], (5, 6, 7))):
        pos = 0
        table = [0] * slots
        for kap in order:
            first_m = m0 + ((z + d * kap - m0) & 7)
            for e in range(2):
                m = first_m + 8 * e
                present = m < m1
                value = source_index(m - m0)
                for q in range(slots):
                    table[q] = where(present & (pos == q), value, table[q])
                pos = pos + where(present, 1, 0)
        for q in range(slots):
            out[base + q] = table[q]
    total = first(2 * NZ)
    begins = [begin(i) for i in range(NZ + 1)]
    for s in range(PAGES):
        m = 8 * s + z
        zs = 0
        for i in range(NZ - 1):
            zs = zs + where(begins[i + 1] <= m, 1, 0)
        s0, s1 = begins[0], begins[1]
        for i in range(1, NZ):
            s0 = where(zs == i, begins[i], s0)
            s1 = where(zs == i, begins[i + 1], s1)
        kap = (d * (z - zs)) & 7
        second = where(m - 8 >= s0, 1, 0)

        def count(k):
            f = s0 + ((zs + d * k - s0) & 7)
            return where(f < s1, 1, 0) + where(f + 8 < s1, 1, 0)

        value = source_index(m - m0)
        pos = second
        for k in (4, 3, 2, 1):
            value = where(kap == k, BASE_A[k - 1] + pos, value)
            pos = pos + count(k)
        pos = second
        for k in (5, 6, 7):
            value = where(kap == k, BASE_B[7 - k] + pos, value)
            pos = pos + count(k)
        out[T_J + s] = zs >> 1
        out[T_F + s] = where(16 * s + 2 * z + c < total, value, ZERO)
    return out


def table_kernel(len_ref, tab_ref, first_ref):
    t = lax.axis_index("tp")
    z, c = t // 2, t % 2
    running = jnp.int32(0)
    first_ref[0] = running
    for i in range(2 * NZ):
        running = running + ((len_ref[0, i] + (BLK - 1)) >> 7)
        first_ref[i + 1] = running
    out = tables(lambda i: first_ref[i], len_ref[0, t], z, c, jnp.where)
    for i in range(T_SIZE):
        tab_ref[i] = jnp.asarray(out.get(i, 0), I32)


def main_kernel(rows, depth, *refs):
    (tab, wp, kg, cs_hbm, x_hbm, out,
     xv, csv, rs, W, pairb, own, acc, fin, stp, prv, sta, stb,
     ra1, ra2, ra3, ra4, rb1, rb2, rb3,
     x_sem, cs_sem, pair_s, pair_r, z_s, z_r,
     p1_s, p1_r, p1h_s, p1h_r, p2_s, p2_r, p2h_s, p2h_r, h_s, h_r, a2a_s, a2a_r) = refs
    ra, rb = (ra1, ra2, ra3, ra4), (rb1, rb2, rb3)
    half = depth // 32
    quarter = half // 2
    g, t = lax.axis_index("grp"), lax.axis_index("tp")
    z, c = t // 2, t % 2
    y, x = g // 4, g % 4
    d = 1 - 2 * c
    zp = z // 2

    def dev(gg, tt):
        return {"grp": gg, "tp": tt}

    partner = dev(g, t + d)
    z_peers = [dev(g, 2 * (2 * zp + (1 - z % 2)) + c)]
    for k in (1, 2, 3):
        for e in (0, 1):
            z_peers.append(dev(g, 2 * (2 * ((zp + 4 - k) % 4) + e) + c))
    far = dev(g, 2 * ((z + d + NZ) % NZ) + c)
    near = dev(g, 2 * ((z - d + NZ) % NZ) + c)

    def at(a, b):
        yy = (y + jnp.where(c == 0, b, a) + 4) % 4
        xx = (x + jnp.where(c == 0, a, b) + 4) % 4
        return yy, xx

    def peer(a, b):
        yy, xx = at(a, b)
        return dev(yy * 4 + xx, t)

    first = (peer(1, 0), peer(-1, 0))
    second = (peer(0, 1), peer(0, -1))
    offsets = (0, -1, 1, 2)

    def x_copy(b):
        rows_b = pl.ds(pl.multiple_of(b * BLK, BLK), BLK)
        return pltpu.make_async_copy(x_hbm.at[rows_b], xv.at[rows_b], x_sem.at[b])

    cs_copy = pltpu.make_async_copy(cs_hbm, csv, cs_sem)

    @pl.loop(0, NB)
    def _(b):
        x_copy(b).start()

    cs_copy.start()

    barrier = pltpu.get_barrier_semaphore()
    everyone = [partner, *z_peers, *first, *second]
    for p in everyone:
        pl.semaphore_signal(barrier, inc=1, device_id=p, device_id_type=MESH)
    pl.semaphore_wait(barrier, len(everyone))

    def remote(s, r, ss, rr, p):
        return pltpu.make_async_remote_copy(
            src_ref=s, dst_ref=r, send_sem=ss, recv_sem=rr, device_id=p, device_id_type=MESH
        )

    def arrived(ref, sem):
        pltpu.make_async_copy(ref, ref, sem).wait()

    pair_copy = remote(
        wp.at[pl.ds(pl.multiple_of((1 - c) * half, half), half)], pairb, pair_s, pair_r, partner
    )
    pair_copy.start()
    pair_copy.wait_recv()
    mine = wp[pl.ds(pl.multiple_of(c * half, half), half)]
    W[z, y, x, c] = mine + pairb[...]

    def z_copy(k):
        return remote(W.at[z, y, x, c], W.at[z, y, x, c], z_s.at[k], z_r.at[z], z_peers[k])

    for k in range(NZ - 1):
        z_copy(k).start()

    def chunk(s):
        return (zp + s) % NC

    def piece(s, a, b):
        yy, xx = at(a, b)
        return W.at[pl.ds(2 * chunk(s), 2), yy, xx, c]

    def part(s, a, b, h):
        yy, xx = at(a, b)
        return W.at[pl.ds(2 * chunk(s), 2), yy, xx, c, pl.ds(h * quarter, quarter)]

    def p1_copy(s, v):
        return remote(piece(s, 0, 0), piece(s, 0, 0), p1_s.at[s, v], p1_r.at[s, v], first[v])

    def p1h_copy(s, v):
        w = part(s, -1 if v == 0 else 1, 0, v)
        return remote(w, w, p1h_s.at[s, v], p1h_r.at[s, v], first[v])

    def p2_copy(s, v, i):
        w = piece(s, offsets[i], 0)
        return remote(w, w, p2_s.at[s, v, i], p2_r.at[s, v, i], second[v])

    def p2h_copy(s, v, i):
        w = part(s, offsets[i], -1 if v == 0 else 1, v)
        return remote(w, w, p2h_s.at[s, v, i], p2h_r.at[s, v], second[v])

    def hand_copy(s, i, j):
        w = piece(s, offsets[i], offsets[j])
        return remote(w, w, h_s.at[s, i, j], h_r.at[s], partner)

    one = W.at[pl.ds(0, 2), 0, 0, 0]
    one_part = W.at[pl.ds(0, 2), 0, 0, 0, pl.ds(0, quarter)]
    four_parts = W.at[pl.ds(0, 2), 0, :, 0, pl.ds(0, quarter)]
    whole_half = W.at[pl.ds(0, 2), :, :, 0]

    def send_row(s, i):
        for v in range(2):
            p2_copy(s, v, i).start()
        hand_copy(s, i, 0).start()

    def stage1(s, own_pair):
        if own_pair:
            arrived(W.at[0, 0, 0, 0], z_r.at[2 * zp + (1 - z % 2)])
        else:
            for e in range(2):
                arrived(W.at[0, 0, 0, 0], z_r.at[2 * chunk(s) + e])
        for v in range(2):
            p1_copy(s, v).start()
        send_row(s, 0)

    def stage2(s):
        for v in range(2):
            arrived(one, p1_r.at[s, v])
            p1h_copy(s, v).start()
            send_row(s, 1 + v)

    def stage3(s):
        for v in range(2):
            arrived(one_part, p1h_r.at[s, v])
        send_row(s, 3)
        for i in range(4):
            for v in range(2):
                arrived(one, p2_r.at[s, v, i])
                p2h_copy(s, v, i).start()
                hand_copy(s, i, 1 + v).start()

    def stage4(s):
        for v in range(2):
            arrived(four_parts, p2h_r.at[s, v])
        for i in range(4):
            hand_copy(s, i, 3).start()

    length = tab[T_LEN]

    def row_scales(lo, hi):
        @pl.loop(lo, hi)
        def _(b):
            x_copy(b).wait()
            r0 = pl.multiple_of(b * BLK, BLK)
            rows_b = pl.ds(r0, BLK)
            total = jnp.zeros((BLK, HD), F32)
            for k in range(depth // HD):
                v = xv[rows_b, k * HD:(k + 1) * HD].astype(F32)
                total = total + v * v
            mean = jnp.sum(total, axis=1, keepdims=True) * (1.0 / depth)
            scale = jnp.broadcast_to(lax.rsqrt(mean + EPS), (BLK, HD))
            p = r0 + lax.broadcasted_iota(I32, (BLK, HD), 0)
            rs[rows_b, :] = jnp.where(p < length, scale, 0.0)

    stage1(0, True)
    row_scales(0, 2)
    stage2(0)
    row_scales(2, 4)
    stage3(0)
    stage1(1, False)
    row_scales(4, 7)
    stage4(0)
    stage2(1)
    row_scales(7, NB)
    cs_copy.wait()
    for j in range(NC):
        fin[j * NS + ZERO] = jnp.zeros((BLK, CW), BF)

    def compute(j):
        n = chunk(j)
        tile = 3 * BLK

        @pl.loop(0, NB // 3)
        def _(i):
            r0 = pl.multiple_of(i * tile, tile)
            rows_i = pl.ds(r0, tile)
            w = jnp.concatenate(
                [W[2 * n].reshape(depth, HD), W[2 * n + 1].reshape(depth, HD)], axis=1
            )
            a = jnp.dot(xv[rows_i, :], w, preferred_element_type=F32)
            scale = rs[rows_i, :]
            acc[...] = a * jnp.concatenate([scale, scale], axis=1)

            @pl.when(n < NC // 2)
            def _():
                for h in range(2):
                    k = acc[:, h * HD:(h + 1) * HD]
                    s = lax.rsqrt(jnp.mean(k * k, axis=1, keepdims=True) + EPS)
                    k = k * s * kg[...]
                    turned = k * csv[0, rows_i, :] + pltpu.roll(k, HD // 2, 1) * csv[1, rows_i, :]
                    own[pl.ds(3 * i, 3), :, h * HD:(h + 1) * HD] = turned.astype(BF).reshape(3, BLK, HD)

            @pl.when(n >= NC // 2)
            def _():
                own[pl.ds(3 * i, 3)] = acc[...].astype(BF).reshape(3, BLK, CW)

    def pair_block_copy(j):
        return remote(stp.at[j], prv.at[j], a2a_s.at[j, 0], a2a_r.at[j, 0], partner)

    def hop_a(j, h):
        s = sta.at[j] if h == 0 else ra[h - 1].at[j, pl.ds(0, CA[h])]
        return remote(s, ra[h].at[j], a2a_s.at[j, 1 + h], a2a_r.at[j, 1 + h], far)

    def hop_b(j, h):
        s = stb.at[j] if h == 0 else rb[h - 1].at[j, pl.ds(0, CB[h])]
        return remote(s, rb[h].at[j], a2a_s.at[j, 5 + h], a2a_r.at[j, 5 + h], near)

    def send_first(j):
        base = j * NS
        for e in range(5):
            stp[j, e] = own[tab[T_P + e]]
        pair_block_copy(j).start()
        for e in range(5):
            fin[base + e] = own[tab[T_O + e]]
        pair_block_copy(j).wait_recv()
        for e in range(5):
            fin[base + 5 + e] = prv[j, e]
        for q in range(CA[0]):
            sta[j, q] = fin[base + tab[T_A + q]]
        hop_a(j, 0).start()
        for q in range(CB[0]):
            stb[j, q] = fin[base + tab[T_B + q]]
        hop_b(j, 0).start()

    def forward(j, h):
        hop_a(j, h - 1).wait_recv()
        if h < 4:
            hop_a(j, h).start()
        if h < 4:
            hop_b(j, h - 1).wait_recv()
        if h < 3:
            hop_b(j, h).start()
        base = j * NS
        for q in range(CA[h - 1]):
            fin[base + BASE_A[h - 1] + q] = ra[h - 1][j, q]
        if h < 4:
            for q in range(CB[h - 1]):
                fin[base + BASE_B[h - 1] + q] = rb[h - 1][j, q]

    @pl.loop(0, NC + 4)
    def _(j):
        @pl.when(j < NC)
        def _():
            arrived(whole_half, h_r.at[j])

            @pl.when(j + 2 < NC)
            def _():
                stage1(j + 2, False)

            compute(j)

            @pl.when(j + 1 < NC)
            def _():
                stage3(j + 1)

            send_first(j)

            @pl.when(j + 2 < NC)
            def _():
                stage2(j + 2)

        for h in (1, 2, 3, 4):
            @pl.when((j - h >= 0) & (j - h < NC))
            def _():
                forward(j - h, h)

        @pl.when(j + 1 < NC)
        def _():
            stage4(j + 1)

    for s in range(PAGES):
        slot, pair = tab[T_F + s], tab[T_J + s]
        for n in range(NC):
            out[s, :, n * CW:(n + 1) * CW] = fin[((n + NC - pair) % NC) * NS + slot]

    pair_copy.wait_send()
    for k in range(NZ - 1):
        z_copy(k).wait_send()

    @pl.loop(0, NC)
    def _(s):
        for v in range(2):
            p1_copy(s, v).wait_send()
            p1h_copy(s, v).wait_send()
            for i in range(4):
                p2_copy(s, v, i).wait_send()
                p2h_copy(s, v, i).wait_send()
        for i in range(4):
            for j in range(4):
                hand_copy(s, i, j).wait_send()
        pair_block_copy(s).wait_send()
        for h in range(4):
            hop_a(s, h).wait_send()
        for h in range(3):
            hop_b(s, h).wait_send()


def rotary(rows):
    m = np.arange(HD // 2, dtype=np.float64)
    angle = np.arange(rows, dtype=np.float64)[:, None] * (1000000.0 ** (-2.0 * m / HD))[None, :]
    cos, sin = np.cos(angle), np.sin(angle)
    return np.stack([np.concatenate([cos, cos], 1), np.concatenate([-sin, sin], 1)]).astype(np.float32)


def local(hidden, lengths, kv_weight, input_gain, key_gain):
    rows, depth = hidden.shape
    piece = depth // 16
    g, t = lax.axis_index("grp"), lax.axis_index("tp")
    vm, sm, anym = (pl.BlockSpec(memory_space=s) for s in (pltpu.VMEM, pltpu.SMEM, pl.ANY))
    tab = pl.pallas_call(
        table_kernel,
        out_shape=jax.ShapeDtypeStruct((T_SIZE,), I32),
        in_specs=[sm],
        out_specs=sm,
        scratch_shapes=[pltpu.SMEM((2 * NZ + 1,), I32)],
        name="tables",
    )(lengths)
    gain = lax.dynamic_slice(input_gain, (g * piece,), (piece,))
    scaled = (kv_weight.astype(F32) * gain[:, None]).astype(BF)
    lane = lax.broadcasted_iota(I32, (piece, HD), 1) // (HD // 2)
    wp = jnp.where(lane == t % 2, jnp.concatenate([scaled, scaled], axis=1), jnp.zeros((), BF))
    blk = lambda *s: pltpu.VMEM((*s, BLK, CW), BF)
    dma = lambda *s: pltpu.SemaphoreType.DMA(s)
    half = piece // 2
    return pl.pallas_call(
        functools.partial(main_kernel, rows, depth),
        out_shape=jax.ShapeDtypeStruct((PAGES, BLK, NC * CW), BF),
        in_specs=[sm, vm, vm, anym, anym],
        out_specs=vm,
        scratch_shapes=[
            pltpu.VMEM((rows, depth), BF),
            pltpu.VMEM((2, rows, HD), F32),
            pltpu.VMEM((rows, HD), F32),
            pltpu.VMEM((NZ, 4, 4, 2, half, HD), BF),
            pltpu.VMEM((half, HD), BF),
            blk(NB),
            pltpu.VMEM((3 * BLK, CW), F32),
            blk(NC * NS),
            blk(NC, 5),
            blk(NC, 5),
            blk(NC, CA[0]),
            blk(NC, CB[0]),
            *[blk(NC, s) for s in CA],
            *[blk(NC, s) for s in CB],
            dma(NB),
            *[pltpu.SemaphoreType.DMA] * 3,
            dma(NZ - 1),
            dma(NZ),
            *[dma(NC, 2)] * 4,
            *[dma(NC, 2, 4)] * 3,
            dma(NC, 2),
            dma(NC, 4, 4),
            dma(NC),
            dma(NC, 8),
            dma(NC, 8),
        ],
        compiler_params=pltpu.CompilerParams(
            collective_id=0, has_side_effects=True, vmem_limit_bytes=66_000_000
        ),
        name="recompute",
    )(tab, wp, key_gain[None, :], jnp.asarray(rotary(rows)), hidden)


def solution(mesh):
    placed = (P(("grp", "tp"), None), P("grp", None), P("grp", "tp"), P(), P())
    return jax.shard_map(
        local,
        mesh=mesh,
        in_specs=placed,
        out_specs=P(("grp", "tp"), None, None),
        check_vma=False,
    )
```

```python
import functools
import math

import jax
import jax.numpy as jnp
import numpy as np
from jax import lax
from jax.experimental import pallas as pl
from jax.experimental.pallas import tpu as pltpu
from jax.sharding import PartitionSpec as P

HD = 128
BLK = 128
NB = 9
NZ = 8
PAGES = 5
NC = 8
CW = 128
EPS = 1e-06
MESH = pl.DeviceIdType.MESH
BF, F32, I32 = jnp.bfloat16, jnp.float32, jnp.int32

CA = (5, 4, 3, 2)
CB = (4, 3, 2)
SRC = 10
BASE_A = tuple(SRC + sum(CA[:i]) for i in range(4))
BASE_B = tuple(SRC + sum(CA) + sum(CB[:i]) for i in range(3))
ZERO = SRC + sum(CA) + sum(CB)
NS = ZERO + 1
T_LEN, T_P, T_O, T_A, T_B, T_F, T_J = 0, 1, 6, 11, 16, 20, 25
T_SIZE = 32


def tables(first, length, z, c, where):
    d = 1 - 2 * c
    seq = 2 * z + c

    def begin(zz):
        return (first(2 * zz) - c + 1) >> 1

    out = {T_LEN: length}
    fs = first(seq)
    for e in range(5):
        b = ((fs + 1 - c) & 1) + 2 * e
        out[T_P + e] = where(b > NB - 1, NB - 1, b)
        b = ((fs + c) & 1) + 2 * e
        out[T_O + e] = where(b > NB - 1, NB - 1, b)
    m0, m1 = begin(z), begin(z + 1)
    q0 = ((first(2 * z + 1) - c + 1) >> 1) - m0

    def source_index(u):
        lead = u < q0
        v = where(c == 0, where(lead, u, 5 + u - q0), where(lead, 5 + u, u - q0))
        v = where(v < 0, 0, v)
        return where(v > SRC - 1, SRC - 1, v)

    for base, slots, order in ((T_A, CA[0], (4, 3, 2, 1)), (T_B, CB[0], (5, 6, 7))):
        pos = 0
        table = [0] * slots
        for kap in order:
            first_m = m0 + ((z + d * kap - m0) & 7)
            for e in range(2):
                m = first_m + 8 * e
                present = m < m1
                value = source_index(m - m0)
                for q in range(slots):
                    table[q] = where(present & (pos == q), value, table[q])
                pos = pos + where(present, 1, 0)
        for q in range(slots):
            out[base + q] = table[q]
    total = first(2 * NZ)
    begins = [begin(i) for i in range(NZ + 1)]
    for s in range(PAGES):
        m = 8 * s + z
        zs = 0
        for i in range(NZ - 1):
            zs = zs + where(begins[i + 1] <= m, 1, 0)
        s0, s1 = begins[0], begins[1]
        for i in range(1, NZ):
            s0 = where(zs == i, begins[i], s0)
            s1 = where(zs == i, begins[i + 1], s1)
        kap = (d * (z - zs)) & 7
        second = where(m - 8 >= s0, 1, 0)

        def count(k):
            f = s0 + ((zs + d * k - s0) & 7)
            return where(f < s1, 1, 0) + where(f + 8 < s1, 1, 0)

        value = source_index(m - m0)
        pos = second
        for k in (4, 3, 2, 1):
            value = where(kap == k, BASE_A[k - 1] + pos, value)
            pos = pos + count(k)
        pos = second
        for k in (5, 6, 7):
            value = where(kap == k, BASE_B[7 - k] + pos, value)
            pos = pos + count(k)
        out[T_J + s] = zs
        out[T_F + s] = where(16 * s + 2 * z + c < total, value, ZERO)
    return out


def table_kernel(len_ref, tab_ref, first_ref):
    t = lax.axis_index("tp")
    z, c = t // 2, t % 2
    running = jnp.int32(0)
    first_ref[0] = running
    for i in range(2 * NZ):
        running = running + ((len_ref[0, i] + (BLK - 1)) >> 7)
        first_ref[i + 1] = running
    out = tables(lambda i: first_ref[i], len_ref[0, t], z, c, jnp.where)
    for i in range(T_SIZE):
        tab_ref[i] = jnp.asarray(out.get(i, 0), I32)


def main_kernel(rows, depth, *refs):
    (tab, wt, gain, kg, cs_hbm, x_hbm, out,
     xv, csv, rs, W, turn, wp, pairb, own, acc, fin, stp, prv, sta, stb,
     ra1, ra2, ra3, ra4, rb1, rb2, rb3,
     x_sem, cs_sem, pair_s, pair_r, z_s, z_r,
     p1_s, p1_r, p1h_s, p1h_r, p2_s, p2_r, p2h_s, p2h_r, h_s, h_r, a2a_s, a2a_r) = refs
    ra, rb = (ra1, ra2, ra3, ra4), (rb1, rb2, rb3)
    half = depth // 32
    quarter = half // 2
    g, t = lax.axis_index("grp"), lax.axis_index("tp")
    z, c = t // 2, t % 2
    y, x = g // 4, g % 4
    d = 1 - 2 * c

    def dev(gg, tt):
        return {"grp": gg, "tp": tt}

    partner = dev(g, t + d)
    above, below = dev(g, 2 * ((z + 1) % NZ) + c), dev(g, 2 * ((z + NZ - 1) % NZ) + c)
    far = dev(g, 2 * ((z + d + NZ) % NZ) + c)
    near = dev(g, 2 * ((z - d + NZ) % NZ) + c)

    def at(a, b):
        yy = (y + jnp.where(c == 0, b, a) + 4) % 4
        xx = (x + jnp.where(c == 0, a, b) + 4) % 4
        return yy, xx

    def peer(a, b):
        yy, xx = at(a, b)
        return dev(yy * 4 + xx, t)

    first = (peer(1, 0), peer(-1, 0))
    second = (peer(0, 1), peer(0, -1))
    offsets = (0, -1, 1, 2)

    def x_copy(b):
        rows_b = pl.ds(pl.multiple_of(b * BLK, BLK), BLK)
        return pltpu.make_async_copy(x_hbm.at[rows_b], xv.at[rows_b], x_sem.at[b])

    cs_copy = pltpu.make_async_copy(cs_hbm, csv, cs_sem)

    @pl.loop(0, NB)
    def _(b):
        x_copy(b).start()

    cs_copy.start()

    barrier = pltpu.get_barrier_semaphore()
    everyone = [partner, above, below, *first, *second]
    for p in everyone:
        pl.semaphore_signal(barrier, inc=1, device_id=p, device_id_type=MESH)

    piece_k = depth // 16
    odd = (g * piece_k) % HD
    window = gain[:, pl.ds(pl.multiple_of(g * piece_k - odd, HD), piece_k + HD // 2)]
    window = jnp.where(odd == 0, window, pltpu.roll(window, piece_k, 1))
    turn[...] = jnp.zeros_like(turn)
    scaled = wt[...].astype(F32) * window[:, :piece_k]
    turn[pl.ds(pl.multiple_of(c * (HD // 2), HD // 2), HD // 2), :piece_k] = scaled
    wp[...] = turn[...].T[:piece_k].astype(BF)

    pl.semaphore_wait(barrier, len(everyone))

    def remote(s, r, ss, rr, p):
        return pltpu.make_async_remote_copy(
            src_ref=s, dst_ref=r, send_sem=ss, recv_sem=rr, device_id=p, device_id_type=MESH
        )

    def arrived(ref, sem):
        pltpu.make_async_copy(ref, ref, sem).wait()

    pair_copy = remote(
        wp.at[pl.ds(pl.multiple_of((1 - c) * half, half), half)], pairb, pair_s, pair_r, partner
    )
    pair_copy.start()
    pair_copy.wait_recv()
    mine = wp[pl.ds(pl.multiple_of(c * half, half), half)]
    W[z, y, x, c] = mine + pairb[...]

    def unit(s):
        return (z + jnp.where(s % 2 == 1, (s + 1) // 2, NZ - s // 2)) % NZ

    def piece(s, a, b):
        yy, xx = at(a, b)
        return W.at[unit(s), yy, xx, c]

    def part(s, a, b, h):
        yy, xx = at(a, b)
        return W.at[unit(s), yy, xx, c, pl.ds(h * quarter, quarter)]

    def p1_copy(s, v):
        return remote(piece(s, 0, 0), piece(s, 0, 0), p1_s.at[s, v], p1_r.at[s, v], first[v])

    def p1h_copy(s, v):
        w = part(s, -1 if v == 0 else 1, 0, v)
        return remote(w, w, p1h_s.at[s, v], p1h_r.at[s, v], first[v])

    def p2_copy(s, v, i):
        w = piece(s, offsets[i], 0)
        return remote(w, w, p2_s.at[s, v, i], p2_r.at[s, v, i], second[v])

    def p2h_copy(s, v, i):
        w = part(s, offsets[i], -1 if v == 0 else 1, v)
        return remote(w, w, p2h_s.at[s, v, i], p2h_r.at[s, v], second[v])

    def hand_copy(s, i, j):
        w = piece(s, offsets[i], offsets[j])
        return remote(w, w, h_s.at[s, i, j], h_r.at[s], partner)

    one = W.at[0, 0, 0, 0]
    one_part = W.at[0, 0, 0, 0, pl.ds(0, quarter)]
    four_parts = W.at[0, 0, :, 0, pl.ds(0, quarter)]
    whole_half = W.at[0, :, :, 0]

    def send_row(s, i):
        for v in range(2):
            p2_copy(s, v, i).start()
        hand_copy(s, i, 0).start()

    def z_pass(s, to, up):
        w = W.at[unit(s), y, x, c]
        return remote(w, w, z_s.at[to], z_r.at[to], above if up else below)

    def stage1(s):
        for v in range(2):
            p1_copy(s, v).start()
        send_row(s, 0)

    def z_step(s):
        arrived(one, z_r.at[s])

        @pl.when((s % 2 == 1) & (s + 2 < NC))
        def _():
            z_pass(s, s + 2, False).start()

        @pl.when((s % 2 == 0) & (s + 2 < NC))
        def _():
            z_pass(s, s + 2, True).start()

        stage1(s)

    def stage2(s):
        for v in range(2):
            arrived(one, p1_r.at[s, v])
            p1h_copy(s, v).start()
            send_row(s, 1 + v)

    def stage3(s):
        for v in range(2):
            arrived(one_part, p1h_r.at[s, v])
        send_row(s, 3)
        for i in range(4):
            for v in range(2):
                arrived(one, p2_r.at[s, v, i])
                p2h_copy(s, v, i).start()
                hand_copy(s, i, 1 + v).start()

    def stage4(s):
        for v in range(2):
            arrived(four_parts, p2h_r.at[s, v])
        for i in range(4):
            hand_copy(s, i, 3).start()

    length = tab[T_LEN]

    def row_scales(lo, hi):
        @pl.loop(lo, hi)
        def _(b):
            x_copy(b).wait()
            r0 = pl.multiple_of(b * BLK, BLK)
            rows_b = pl.ds(r0, BLK)
            total = jnp.zeros((BLK, HD), F32)
            for k in range(depth // HD):
                v = xv[rows_b, k * HD:(k + 1) * HD].astype(F32)
                total = total + v * v
            mean = jnp.sum(total, axis=1, keepdims=True) * (1.0 / depth)
            scale = jnp.broadcast_to(lax.rsqrt(mean + EPS), (BLK, HD))
            p = r0 + lax.broadcasted_iota(I32, (BLK, HD), 0)
            rs[rows_b, :] = jnp.where(p < length, scale, 0.0)

    z_pass(0, 1, False).start()
    z_pass(0, 2, True).start()
    stage1(0)
    row_scales(0, 2)
    stage2(0)
    row_scales(2, 4)
    stage3(0)
    z_step(1)
    row_scales(4, 6)
    stage4(0)
    stage2(1)
    row_scales(6, NB)
    cs_copy.wait()
    for j in range(NC):
        fin[j * NS + ZERO] = jnp.zeros((BLK, CW), BF)

    def compute(j):
        n = unit(j)
        tile = 3 * BLK

        @pl.loop(0, NB // 3)
        def _(i):
            r0 = pl.multiple_of(i * tile, tile)
            rows_i = pl.ds(r0, tile)
            a = jnp.dot(xv[rows_i, :], W[n].reshape(depth, HD), preferred_element_type=F32)
            acc[...] = a * rs[rows_i, :]

            @pl.when(n < NC // 2)
            def _():
                k = acc[...]
                s = lax.rsqrt(jnp.mean(k * k, axis=1, keepdims=True) + EPS)
                k = k * s * kg[...]
                turned = k * csv[0, rows_i, :] + pltpu.roll(k, HD // 2, 1) * csv[1, rows_i, :]
                own[pl.ds(3 * i, 3)] = turned.astype(BF).reshape(3, BLK, HD)

            @pl.when(n >= NC // 2)
            def _():
                own[pl.ds(3 * i, 3)] = acc[...].astype(BF).reshape(3, BLK, CW)

    def pair_block_copy(j):
        return remote(stp.at[j], prv.at[j], a2a_s.at[j, 0], a2a_r.at[j, 0], partner)

    def hop_a(j, h):
        s = sta.at[j] if h == 0 else ra[h - 1].at[j, pl.ds(0, CA[h])]
        return remote(s, ra[h].at[j], a2a_s.at[j, 1 + h], a2a_r.at[j, 1 + h], far)

    def hop_b(j, h):
        s = stb.at[j] if h == 0 else rb[h - 1].at[j, pl.ds(0, CB[h])]
        return remote(s, rb[h].at[j], a2a_s.at[j, 5 + h], a2a_r.at[j, 5 + h], near)

    def send_first(j):
        base = j * NS
        for e in range(5):
            stp[j, e] = own[tab[T_P + e]]
        pair_block_copy(j).start()
        for e in range(5):
            fin[base + e] = own[tab[T_O + e]]
        pair_block_copy(j).wait_recv()
        for e in range(5):
            fin[base + 5 + e] = prv[j, e]
        for q in range(CA[0]):
            sta[j, q] = fin[base + tab[T_A + q]]
        hop_a(j, 0).start()
        for q in range(CB[0]):
            stb[j, q] = fin[base + tab[T_B + q]]
        hop_b(j, 0).start()

    def forward(j, h):
        hop_a(j, h - 1).wait_recv()
        if h < 4:
            hop_a(j, h).start()
        if h < 4:
            hop_b(j, h - 1).wait_recv()
        if h < 3:
            hop_b(j, h).start()
        base = j * NS
        for q in range(CA[h - 1]):
            fin[base + BASE_A[h - 1] + q] = ra[h - 1][j, q]
        if h < 4:
            for q in range(CB[h - 1]):
                fin[base + BASE_B[h - 1] + q] = rb[h - 1][j, q]

    @pl.loop(0, NC + 4)
    def _(j):
        @pl.when(j < NC)
        def _():
            arrived(whole_half, h_r.at[j])

            @pl.when(j + 2 < NC)
            def _():
                z_step(j + 2)

            compute(j)
            send_first(j)

            @pl.when(j + 1 < NC)
            def _():
                stage3(j + 1)

            @pl.when(j + 2 < NC)
            def _():
                stage2(j + 2)

        for h in (1, 2, 3, 4):
            @pl.when((j - h >= 0) & (j - h < NC))
            def _():
                forward(j - h, h)

        @pl.when(j + 1 < NC)
        def _():
            stage4(j + 1)

    for p in range(PAGES):
        slot, chip = tab[T_F + p], tab[T_J + p]
        for n in range(NC):
            o = (n + NZ - chip) % NZ
            s = jnp.where(o == 0, 0, jnp.where(o <= NZ // 2, 2 * o - 1, 2 * (NZ - o)))
            out[p, :, n * CW:(n + 1) * CW] = fin[s * NS + slot]

    pair_copy.wait_send()
    for k in range(1, NC):
        arrived(one, z_s.at[k])

    @pl.loop(0, NC)
    def _(s):
        for v in range(2):
            p1_copy(s, v).wait_send()
            p1h_copy(s, v).wait_send()
            for i in range(4):
                p2_copy(s, v, i).wait_send()
                p2h_copy(s, v, i).wait_send()
        for i in range(4):
            for j in range(4):
                hand_copy(s, i, j).wait_send()
        pair_block_copy(s).wait_send()
        for h in range(4):
            hop_a(s, h).wait_send()
        for h in range(3):
            hop_b(s, h).wait_send()


def rotary(rows):
    m = np.arange(HD // 2, dtype=np.float64)
    angle = np.arange(rows, dtype=np.float64)[:, None] * (1000000.0 ** (-2.0 * m / HD))[None, :]
    cos, sin = np.cos(angle), np.sin(angle)
    return np.stack([np.concatenate([cos, cos], 1), np.concatenate([-sin, sin], 1)]).astype(np.float32)


def local(hidden, lengths, kv_weight, input_gain, key_gain):
    rows, depth = hidden.shape
    piece = depth // 16
    vm, sm, anym = (pl.BlockSpec(memory_space=s) for s in (pltpu.VMEM, pltpu.SMEM, pl.ANY))
    tab = pl.pallas_call(
        table_kernel,
        out_shape=jax.ShapeDtypeStruct((T_SIZE,), I32),
        in_specs=[sm],
        out_specs=sm,
        scratch_shapes=[pltpu.SMEM((2 * NZ + 1,), I32)],
        name="tables",
    )(lengths)
    blk = lambda *s: pltpu.VMEM((*s, BLK, CW), BF)
    dma = lambda *s: pltpu.SemaphoreType.DMA(s)
    half = piece // 2
    pages = pl.pallas_call(
        functools.partial(main_kernel, rows, depth),
        out_shape=jax.ShapeDtypeStruct((PAGES, BLK, NC * CW), BF),
        in_specs=[sm, vm, vm, vm, anym, anym],
        out_specs=vm,
        scratch_shapes=[
            pltpu.VMEM((rows, depth), BF),
            pltpu.VMEM((2, rows, HD), F32),
            pltpu.VMEM((rows, HD), F32),
            pltpu.VMEM((NZ, 4, 4, 2, half, HD), BF),
            pltpu.VMEM((HD, piece + HD // 2), F32),
            pltpu.VMEM((piece, HD), BF),
            pltpu.VMEM((half, HD), BF),
            blk(NB),
            pltpu.VMEM((3 * BLK, CW), F32),
            blk(NC * NS),
            blk(NC, 5),
            blk(NC, 5),
            blk(NC, CA[0]),
            blk(NC, CB[0]),
            *[blk(NC, s) for s in CA],
            *[blk(NC, s) for s in CB],
            dma(NB),
            *[pltpu.SemaphoreType.DMA] * 3,
            dma(NC),
            dma(NC),
            *[dma(NC, 2)] * 4,
            *[dma(NC, 2, 4)] * 3,
            dma(NC, 2),
            dma(NC, 4, 4),
            dma(NC),
            dma(NC, 8),
            dma(NC, 8),
        ],
        compiler_params=pltpu.CompilerParams(
            collective_id=0, has_side_effects=True, vmem_limit_bytes=66_000_000
        ),
        name="recompute",
    )(tab, kv_weight.T, input_gain[None, :], key_gain[None, :], jnp.asarray(rotary(rows)), hidden)
    live = tab[T_F:T_F + PAGES] != ZERO
    return jnp.where(live[:, None, None], pages, jnp.zeros((), BF))


def solution(mesh):
    placed = (P(("grp", "tp"), None), P("grp", None), P("grp", "tp"), P(), P())
    return jax.shard_map(
        local,
        mesh=mesh,
        in_specs=placed,
        out_specs=P(("grp", "tp"), None, None),
        check_vma=False,
    )
```

```python
import functools
import math

import jax
import jax.numpy as jnp
import numpy as np
from jax import lax
from jax.experimental import pallas as pl
from jax.experimental.pallas import tpu as pltpu
from jax.sharding import PartitionSpec as P

HD = 128
BLK = 128
NB = 9
NZ = 8
PAGES = 5
NC = 8
CW = 128
EPS = 1e-06
MESH = pl.DeviceIdType.MESH
BF, F32, I32 = jnp.bfloat16, jnp.float32, jnp.int32

CA = (5, 4, 3, 2)
CB = (4, 3, 2)
SRC = 10
BASE_A = tuple(SRC + sum(CA[:i]) for i in range(4))
BASE_B = tuple(SRC + sum(CA) + sum(CB[:i]) for i in range(3))
ZERO = SRC + sum(CA) + sum(CB)
NS = ZERO + 1
T_LEN, T_P, T_O, T_A, T_B, T_F, T_J = 0, 1, 6, 11, 16, 20, 25
T_SIZE = 32


def tables(first, length, z, c, where):
    d = 1 - 2 * c
    seq = 2 * z + c

    def begin(zz):
        return (first(2 * zz) - c + 1) >> 1

    out = {T_LEN: length}
    fs = first(seq)
    for e in range(5):
        b = ((fs + 1 - c) & 1) + 2 * e
        out[T_P + e] = where(b > NB - 1, NB - 1, b)
        b = ((fs + c) & 1) + 2 * e
        out[T_O + e] = where(b > NB - 1, NB - 1, b)
    m0, m1 = begin(z), begin(z + 1)
    q0 = ((first(2 * z + 1) - c + 1) >> 1) - m0

    def source_index(u):
        lead = u < q0
        v = where(c == 0, where(lead, u, 5 + u - q0), where(lead, 5 + u, u - q0))
        v = where(v < 0, 0, v)
        return where(v > SRC - 1, SRC - 1, v)

    for base, slots, order in ((T_A, CA[0], (4, 3, 2, 1)), (T_B, CB[0], (5, 6, 7))):
        pos = 0
        table = [0] * slots
        for kap in order:
            first_m = m0 + ((z + d * kap - m0) & 7)
            for e in range(2):
                m = first_m + 8 * e
                present = m < m1
                value = source_index(m - m0)
                for q in range(slots):
                    table[q] = where(present & (pos == q), value, table[q])
                pos = pos + where(present, 1, 0)
        for q in range(slots):
            out[base + q] = table[q]
    total = first(2 * NZ)
    begins = [begin(i) for i in range(NZ + 1)]
    for s in range(PAGES):
        m = 8 * s + z
        zs = 0
        for i in range(NZ - 1):
            zs = zs + where(begins[i + 1] <= m, 1, 0)
        s0, s1 = begins[0], begins[1]
        for i in range(1, NZ):
            s0 = where(zs == i, begins[i], s0)
            s1 = where(zs == i, begins[i + 1], s1)
        kap = (d * (z - zs)) & 7
        second = where(m - 8 >= s0, 1, 0)

        def count(k):
            f = s0 + ((zs + d * k - s0) & 7)
            return where(f < s1, 1, 0) + where(f + 8 < s1, 1, 0)

        value = source_index(m - m0)
        pos = second
        for k in (4, 3, 2, 1):
            value = where(kap == k, BASE_A[k - 1] + pos, value)
            pos = pos + count(k)
        pos = second
        for k in (5, 6, 7):
            value = where(kap == k, BASE_B[7 - k] + pos, value)
            pos = pos + count(k)
        out[T_J + s] = zs
        out[T_F + s] = where(16 * s + 2 * z + c < total, value, ZERO)
    return out


def table_kernel(len_ref, tab_ref, first_ref):
    t = lax.axis_index("tp")
    z, c = t // 2, t % 2
    running = jnp.int32(0)
    first_ref[0] = running
    for i in range(2 * NZ):
        running = running + ((len_ref[0, i] + (BLK - 1)) >> 7)
        first_ref[i + 1] = running
    out = tables(lambda i: first_ref[i], len_ref[0, t], z, c, jnp.where)
    for i in range(T_SIZE):
        tab_ref[i] = jnp.asarray(out.get(i, 0), I32)


def main_kernel(rows, depth, *refs):
    (tab, wt, gain, kg, cs_hbm, x_hbm, out,
     xv, csv, rs, W, turn, wp, pairb, own, acc, fin, stp, prv, sta, stb,
     ra1, ra2, ra3, ra4, rb1, rb2, rb3,
     x_sem, cs_sem, pair_s, pair_r, z_s, z_r,
     p1_s, p1_r, p1h_s, p1h_r, p2_s, p2_r, p2h_s, p2h_r, h_s, h_r, a2a_s, a2a_r) = refs
    ra, rb = (ra1, ra2, ra3, ra4), (rb1, rb2, rb3)
    half = depth // 32
    quarter = half // 2
    g, t = lax.axis_index("grp"), lax.axis_index("tp")
    z, c = t // 2, t % 2
    y, x = g // 4, g % 4
    d = 1 - 2 * c

    def dev(gg, tt):
        return {"grp": gg, "tp": tt}

    partner = dev(g, t + d)
    above, below = dev(g, 2 * ((z + 1) % NZ) + c), dev(g, 2 * ((z + NZ - 1) % NZ) + c)
    far = dev(g, 2 * ((z + d + NZ) % NZ) + c)
    near = dev(g, 2 * ((z - d + NZ) % NZ) + c)

    p, q = jnp.where(c == 0, x, y), jnp.where(c == 0, y, x)

    def peer(i, j):
        i, j = (p + i + 4) % 4, (q + j + 4) % 4
        return dev(jnp.where(c == 0, j * 4 + i, i * 4 + j), t)

    first = (peer(1, 0), peer(-1, 0))
    second = (peer(0, 1), peer(0, -1))

    def x_copy(b):
        rows_b = pl.ds(pl.multiple_of(b * BLK, BLK), BLK)
        return pltpu.make_async_copy(x_hbm.at[rows_b], xv.at[rows_b], x_sem.at[b])

    cs_copy = pltpu.make_async_copy(cs_hbm, csv, cs_sem)

    @pl.loop(0, NB)
    def _(b):
        x_copy(b).start()

    cs_copy.start()

    barrier = pltpu.get_barrier_semaphore()
    everyone = [partner, above, below, *first, *second]
    for other in everyone:
        pl.semaphore_signal(barrier, inc=1, device_id=other, device_id_type=MESH)

    piece_k = depth // 16
    odd = (g * piece_k) % HD
    window = gain[:, pl.ds(pl.multiple_of(g * piece_k - odd, HD), piece_k + HD // 2)]
    window = jnp.where(odd == 0, window, pltpu.roll(window, piece_k, 1))
    turn[...] = jnp.zeros_like(turn)
    scaled = wt[...].astype(F32) * window[:, :piece_k]
    turn[pl.ds(pl.multiple_of(c * (HD // 2), HD // 2), HD // 2), :piece_k] = scaled
    wp[...] = turn[...].T[:piece_k].astype(BF)

    pl.semaphore_wait(barrier, len(everyone))

    def remote(s, r, ss, rr, p):
        return pltpu.make_async_remote_copy(
            src_ref=s, dst_ref=r, send_sem=ss, recv_sem=rr, device_id=p, device_id_type=MESH
        )

    def arrived(ref, sem):
        pltpu.make_async_copy(ref, ref, sem).wait()

    pair_copy = remote(
        wp.at[pl.ds(pl.multiple_of((1 - c) * half, half), half)], pairb, pair_s, pair_r, partner
    )
    pair_copy.start()
    pair_copy.wait_recv()
    mine = wp[pl.ds(pl.multiple_of(c * half, half), half)]
    W[z, c, q, p] = mine + pairb[...]

    def unit(s):
        return (z + jnp.where(s % 2 == 1, (s + 1) // 2, NZ - s // 2)) % NZ

    def piece(s, i):
        return W.at[unit(s), c, q, (p + i + 4) % 4]

    def row(s, j):
        return W.at[unit(s), c, (q + j + 4) % 4]

    def p1_copy(s, v):
        return remote(piece(s, 0), piece(s, 0), p1_s.at[s, v], p1_r.at[s, v], first[v])

    def p1h_copy(s, v):
        w = piece(s, 2 * v - 1).at[pl.ds(v * quarter, quarter)]
        return remote(w, w, p1h_s.at[s, v], p1h_r.at[s, v], first[v])

    def p2_copy(s, v):
        return remote(row(s, 0), row(s, 0), p2_s.at[s, v], p2_r.at[s, v], second[v])

    def p2h_copy(s, v):
        w = row(s, 2 * v - 1).at[pl.ds(2 * v, 2)]
        return remote(w, w, p2h_s.at[s, v], p2h_r.at[s, v], second[v])

    def hand_copy(s, j):
        return remote(row(s, j), row(s, j), h_s.at[s, j + 1], h_r.at[s], partner)

    one = W.at[0, 0, 0, 0]
    one_part = one.at[pl.ds(0, quarter)]
    one_row = W.at[0, 0, 0]
    two = W.at[0, 0, 0, pl.ds(0, 2)]
    whole_half = W.at[0, 0]

    def z_pass(s, to, up):
        return remote(piece(s, 0), piece(s, 0), z_s.at[to], z_r.at[to], above if up else below)

    def stage1(s):
        for v in range(2):
            p1_copy(s, v).start()

    def z_step(s):
        arrived(one, z_r.at[s])
        stage1(s)

        @pl.when((s % 2 == 1) & (s + 2 < NC))
        def _():
            z_pass(s, s + 2, False).start()

        @pl.when((s % 2 == 0) & (s + 2 < NC))
        def _():
            z_pass(s, s + 2, True).start()

    def stage2(s):
        for v in range(2):
            arrived(one, p1_r.at[s, v])
            p1h_copy(s, v).start()

    def stage3(s):
        for v in range(2):
            arrived(one_part, p1h_r.at[s, v])
        for v in range(2):
            p2_copy(s, v).start()
        hand_copy(s, 0).start()

    def stage4(s):
        for v in range(2):
            arrived(one_row, p2_r.at[s, v])
            p2h_copy(s, v).start()
            hand_copy(s, 2 * v - 1).start()

    def stage5(s):
        for v in range(2):
            arrived(two, p2h_r.at[s, v])
        hand_copy(s, 2).start()

    length = tab[T_LEN]

    def row_scales(lo, hi):
        @pl.loop(lo, hi)
        def _(b):
            x_copy(b).wait()
            r0 = pl.multiple_of(b * BLK, BLK)
            rows_b = pl.ds(r0, BLK)
            total = jnp.zeros((BLK, HD), F32)
            for k in range(depth // HD):
                v = xv[rows_b, k * HD:(k + 1) * HD].astype(F32)
                total = total + v * v
            mean = jnp.sum(total, axis=1, keepdims=True) * (1.0 / depth)
            scale = jnp.broadcast_to(lax.rsqrt(mean + EPS), (BLK, HD))
            p = r0 + lax.broadcasted_iota(I32, (BLK, HD), 0)
            rs[rows_b, :] = jnp.where(p < length, scale, 0.0)

    stage1(0)
    z_pass(0, 1, False).start()
    z_pass(0, 2, True).start()
    row_scales(0, 2)
    stage2(0)
    z_step(1)
    row_scales(2, 4)
    stage3(0)
    stage2(1)
    row_scales(4, 6)
    stage4(0)
    stage3(1)
    z_step(2)
    row_scales(6, NB)
    stage5(0)
    stage4(1)
    stage2(2)
    cs_copy.wait()
    for j in range(NC):
        fin[j * NS + ZERO] = jnp.zeros((BLK, CW), BF)

    def compute(j):
        n = unit(j)
        tile = 3 * BLK

        @pl.loop(0, NB // 3)
        def _(i):
            r0 = pl.multiple_of(i * tile, tile)
            rows_i = pl.ds(r0, tile)
            w = [W[n, 0, gg // 4, gg % 4] if cc == 0 else W[n, 1, gg % 4, gg // 4]
                 for gg in range(16) for cc in range(2)]
            a = jnp.dot(xv[rows_i, :], jnp.concatenate(w, axis=0), preferred_element_type=F32)
            acc[...] = a * rs[rows_i, :]

            @pl.when(n < NC // 2)
            def _():
                k = acc[...]
                s = lax.rsqrt(jnp.mean(k * k, axis=1, keepdims=True) + EPS)
                k = k * s * kg[...]
                turned = k * csv[0, rows_i, :] + pltpu.roll(k, HD // 2, 1) * csv[1, rows_i, :]
                own[pl.ds(3 * i, 3)] = turned.astype(BF).reshape(3, BLK, HD)

            @pl.when(n >= NC // 2)
            def _():
                own[pl.ds(3 * i, 3)] = acc[...].astype(BF).reshape(3, BLK, CW)

    def pair_block_copy(j):
        return remote(stp.at[j], prv.at[j], a2a_s.at[j, 0], a2a_r.at[j, 0], partner)

    def hop_a(j, h):
        s = sta.at[j] if h == 0 else ra[h - 1].at[j, pl.ds(0, CA[h])]
        return remote(s, ra[h].at[j], a2a_s.at[j, 1 + h], a2a_r.at[j, 1 + h], far)

    def hop_b(j, h):
        s = stb.at[j] if h == 0 else rb[h - 1].at[j, pl.ds(0, CB[h])]
        return remote(s, rb[h].at[j], a2a_s.at[j, 5 + h], a2a_r.at[j, 5 + h], near)

    def send_pair(j):
        for e in range(5):
            stp[j, e] = own[tab[T_P + e]]
        pair_block_copy(j).start()
        for e in range(5):
            fin[j * NS + e] = own[tab[T_O + e]]

    def send_first(j):
        base = j * NS
        pair_block_copy(j).wait_recv()
        for e in range(5):
            fin[base + 5 + e] = prv[j, e]
        for e in range(CA[0]):
            sta[j, e] = fin[base + tab[T_A + e]]
        hop_a(j, 0).start()
        for e in range(CB[0]):
            stb[j, e] = fin[base + tab[T_B + e]]
        hop_b(j, 0).start()

    def forward(j, h):
        hop_a(j, h - 1).wait_recv()
        if h < 4:
            hop_a(j, h).start()
        if h < 4:
            hop_b(j, h - 1).wait_recv()
        if h < 3:
            hop_b(j, h).start()
        base = j * NS
        for q in range(CA[h - 1]):
            fin[base + BASE_A[h - 1] + q] = ra[h - 1][j, q]
        if h < 4:
            for q in range(CB[h - 1]):
                fin[base + BASE_B[h - 1] + q] = rb[h - 1][j, q]

    def step_in_range(stage, s):
        @pl.when(s < NC)
        def _():
            stage(s)

    @pl.loop(0, NC + 4)
    def _(j):
        @pl.when(j < NC)
        def _():
            arrived(whole_half, h_r.at[j])
            step_in_range(stage5, j + 1)
            step_in_range(stage3, j + 2)
            step_in_range(z_step, j + 3)
            compute(j)
            send_pair(j)
            step_in_range(stage4, j + 2)
            step_in_range(stage2, j + 3)
            send_first(j)

        for h in (1, 2, 3, 4):
            @pl.when((j - h >= 0) & (j - h < NC))
            def _():
                forward(j - h, h)

    for page in range(PAGES):
        slot, chip = tab[T_F + page], tab[T_J + page]
        for n in range(NC):
            o = (n + NZ - chip) % NZ
            s = jnp.where(o == 0, 0, jnp.where(o <= NZ // 2, 2 * o - 1, 2 * (NZ - o)))
            out[page, :, n * CW:(n + 1) * CW] = fin[s * NS + slot]

    pair_copy.wait_send()
    for k in range(1, NC):
        arrived(one, z_s.at[k])

    @pl.loop(0, NC)
    def _(s):
        for v in range(2):
            p1_copy(s, v).wait_send()
            p1h_copy(s, v).wait_send()
            p2_copy(s, v).wait_send()
            p2h_copy(s, v).wait_send()
        for j in (-1, 0, 1, 2):
            hand_copy(s, j).wait_send()
        pair_block_copy(s).wait_send()
        for h in range(4):
            hop_a(s, h).wait_send()
        for h in range(3):
            hop_b(s, h).wait_send()


def rotary(rows):
    m = np.arange(HD // 2, dtype=np.float64)
    angle = np.arange(rows, dtype=np.float64)[:, None] * (1000000.0 ** (-2.0 * m / HD))[None, :]
    cos, sin = np.cos(angle), np.sin(angle)
    return np.stack([np.concatenate([cos, cos], 1), np.concatenate([-sin, sin], 1)]).astype(np.float32)


def local(hidden, lengths, kv_weight, input_gain, key_gain):
    rows, depth = hidden.shape
    piece = depth // 16
    vm, sm, anym = (pl.BlockSpec(memory_space=s) for s in (pltpu.VMEM, pltpu.SMEM, pl.ANY))
    tab = pl.pallas_call(
        table_kernel,
        out_shape=jax.ShapeDtypeStruct((T_SIZE,), I32),
        in_specs=[sm],
        out_specs=sm,
        scratch_shapes=[pltpu.SMEM((2 * NZ + 1,), I32)],
        name="tables",
    )(lengths)
    blk = lambda *s: pltpu.VMEM((*s, BLK, CW), BF)
    dma = lambda *s: pltpu.SemaphoreType.DMA(s)
    half = piece // 2
    pages = pl.pallas_call(
        functools.partial(main_kernel, rows, depth),
        out_shape=jax.ShapeDtypeStruct((PAGES, BLK, NC * CW), BF),
        in_specs=[sm, vm, vm, vm, anym, anym],
        out_specs=vm,
        scratch_shapes=[
            pltpu.VMEM((rows, depth), BF),
            pltpu.VMEM((2, rows, HD), F32),
            pltpu.VMEM((rows, HD), F32),
            pltpu.VMEM((NZ, 2, 4, 4, half, HD), BF),
            pltpu.VMEM((HD, piece + HD // 2), F32),
            pltpu.VMEM((piece, HD), BF),
            pltpu.VMEM((half, HD), BF),
            blk(NB),
            pltpu.VMEM((3 * BLK, CW), F32),
            blk(NC * NS),
            blk(NC, 5),
            blk(NC, 5),
            blk(NC, CA[0]),
            blk(NC, CB[0]),
            *[blk(NC, s) for s in CA],
            *[blk(NC, s) for s in CB],
            dma(NB),
            *[pltpu.SemaphoreType.DMA] * 3,
            dma(NC),
            dma(NC),
            *[dma(NC, 2)] * 8,
            dma(NC, 4),
            dma(NC),
            dma(NC, 8),
            dma(NC, 8),
        ],
        compiler_params=pltpu.CompilerParams(
            collective_id=0, has_side_effects=True, vmem_limit_bytes=66_000_000
        ),
        name="recompute",
    )(tab, kv_weight.T, input_gain[None, :], key_gain[None, :], jnp.asarray(rotary(rows)), hidden)
    live = tab[T_F:T_F + PAGES] != ZERO
    return jnp.where(live[:, None, None], pages, jnp.zeros((), BF))


def solution(mesh):
    placed = (P(("grp", "tp"), None), P("grp", None), P("grp", "tp"), P(), P())
    return jax.shard_map(
        local,
        mesh=mesh,
        in_specs=placed,
        out_specs=P(("grp", "tp"), None, None),
        check_vma=False,
    )
```

```python
import functools
import math

import jax
import jax.numpy as jnp
import numpy as np
from jax import lax
from jax.experimental import pallas as pl
from jax.experimental.pallas import tpu as pltpu
from jax.sharding import PartitionSpec as P

HD = 128
BLK = 128
NB = 9
NZ = 8
PAGES = 5
NC = 8
CW = 128
EPS = 1e-06
MESH = pl.DeviceIdType.MESH
BF, F32, I32 = jnp.bfloat16, jnp.float32, jnp.int32

CA = (5, 4, 3, 2)
CB = (4, 3, 2)
SRC = 10
BASE_A = tuple(SRC + sum(CA[:i]) for i in range(4))
BASE_B = tuple(SRC + sum(CA) + sum(CB[:i]) for i in range(3))
ZERO = SRC + sum(CA) + sum(CB)
NS = ZERO + 1
T_LEN, T_P, T_O, T_A, T_B, T_F, T_J = 0, 1, 6, 11, 16, 20, 25
T_SIZE = 32


def tables(first, length, z, c, where):
    d = 1 - 2 * c
    seq = 2 * z + c

    def begin(zz):
        return (first(2 * zz) - c + 1) >> 1

    out = {T_LEN: length}
    fs = first(seq)
    for e in range(5):
        b = ((fs + 1 - c) & 1) + 2 * e
        out[T_P + e] = where(b > NB - 1, NB - 1, b)
        b = ((fs + c) & 1) + 2 * e
        out[T_O + e] = where(b > NB - 1, NB - 1, b)
    m0, m1 = begin(z), begin(z + 1)
    q0 = ((first(2 * z + 1) - c + 1) >> 1) - m0

    def source_index(u):
        lead = u < q0
        v = where(c == 0, where(lead, u, 5 + u - q0), where(lead, 5 + u, u - q0))
        v = where(v < 0, 0, v)
        return where(v > SRC - 1, SRC - 1, v)

    for base, slots, order in ((T_A, CA[0], (4, 3, 2, 1)), (T_B, CB[0], (5, 6, 7))):
        pos = 0
        table = [0] * slots
        for kap in order:
            first_m = m0 + ((z + d * kap - m0) & 7)
            for e in range(2):
                m = first_m + 8 * e
                present = m < m1
                value = source_index(m - m0)
                for q in range(slots):
                    table[q] = where(present & (pos == q), value, table[q])
                pos = pos + where(present, 1, 0)
        for q in range(slots):
            out[base + q] = table[q]
    total = first(2 * NZ)
    begins = [begin(i) for i in range(NZ + 1)]
    for s in range(PAGES):
        m = 8 * s + z
        zs = 0
        for i in range(NZ - 1):
            zs = zs + where(begins[i + 1] <= m, 1, 0)
        s0, s1 = begins[0], begins[1]
        for i in range(1, NZ):
            s0 = where(zs == i, begins[i], s0)
            s1 = where(zs == i, begins[i + 1], s1)
        kap = (d * (z - zs)) & 7
        second = where(m - 8 >= s0, 1, 0)

        def count(k):
            f = s0 + ((zs + d * k - s0) & 7)
            return where(f < s1, 1, 0) + where(f + 8 < s1, 1, 0)

        value = source_index(m - m0)
        pos = second
        for k in (4, 3, 2, 1):
            value = where(kap == k, BASE_A[k - 1] + pos, value)
            pos = pos + count(k)
        pos = second
        for k in (5, 6, 7):
            value = where(kap == k, BASE_B[7 - k] + pos, value)
            pos = pos + count(k)
        out[T_J + s] = zs
        out[T_F + s] = where(16 * s + 2 * z + c < total, value, ZERO)
    return out


def table_kernel(len_ref, tab_ref, first_ref):
    t = lax.axis_index("tp")
    z, c = t // 2, t % 2
    running = jnp.int32(0)
    first_ref[0] = running
    for i in range(2 * NZ):
        running = running + ((len_ref[0, i] + (BLK - 1)) >> 7)
        first_ref[i + 1] = running
    out = tables(lambda i: first_ref[i], len_ref[0, t], z, c, jnp.where)
    for i in range(T_SIZE):
        tab_ref[i] = jnp.asarray(out.get(i, 0), I32)


def main_kernel(rows, depth, *refs):
    (tab, wt, gain, kg, cs_hbm, x_hbm, out,
     xv, csv, rs, W, turn, wp, pairb, own, acc, fin, stp, prv, sta, stb,
     ra1, ra2, ra3, ra4, rb1, rb2, rb3,
     x_sem, cs_sem, pair_s, pair_r, z_s, z_r,
     p1_s, p1_r, p1h_s, p1h_r, p2_s, p2_r, p2h_s, p2h_r, h_s, h_r, a2a_s, a2a_r) = refs
    ra, rb = (ra1, ra2, ra3, ra4), (rb1, rb2, rb3)
    half = depth // 32
    quarter = half // 2
    g, t = lax.axis_index("grp"), lax.axis_index("tp")
    z, c = t // 2, t % 2
    y, x = g // 4, g % 4
    d = 1 - 2 * c

    def dev(gg, tt):
        return {"grp": gg, "tp": tt}

    partner = dev(g, t + d)
    above, below = dev(g, 2 * ((z + 1) % NZ) + c), dev(g, 2 * ((z + NZ - 1) % NZ) + c)
    far = dev(g, 2 * ((z + d + NZ) % NZ) + c)
    near = dev(g, 2 * ((z - d + NZ) % NZ) + c)

    p, q = jnp.where(c == 0, x, y), jnp.where(c == 0, y, x)

    def peer(i, j):
        i, j = (p + i + 4) % 4, (q + j + 4) % 4
        return dev(jnp.where(c == 0, j * 4 + i, i * 4 + j), t)

    first = (peer(1, 0), peer(-1, 0))
    second = (peer(0, 1), peer(0, -1))

    def x_copy(b):
        rows_b = pl.ds(pl.multiple_of(b * BLK, BLK), BLK)
        return pltpu.make_async_copy(x_hbm.at[rows_b], xv.at[rows_b], x_sem.at[b])

    cs_copy = pltpu.make_async_copy(cs_hbm, csv, cs_sem)

    @pl.loop(0, NB)
    def _(b):
        x_copy(b).start()

    cs_copy.start()

    barrier = pltpu.get_barrier_semaphore()
    everyone = [partner, above, below, *first, *second]
    for other in everyone:
        pl.semaphore_signal(barrier, inc=1, device_id=other, device_id_type=MESH)

    piece_k = depth // 16
    odd = (g * piece_k) % HD
    window = gain[:, pl.ds(pl.multiple_of(g * piece_k - odd, HD), piece_k + HD // 2)]
    window = jnp.where(odd == 0, window, pltpu.roll(window, piece_k, 1))
    turn[...] = jnp.zeros_like(turn)
    scaled = wt[...].astype(F32) * window[:, :piece_k]
    turn[pl.ds(pl.multiple_of(c * (HD // 2), HD // 2), HD // 2), :piece_k] = scaled
    wp[...] = turn[...].T[:piece_k].astype(BF)

    pl.semaphore_wait(barrier, len(everyone))

    def remote(s, r, ss, rr, p):
        return pltpu.make_async_remote_copy(
            src_ref=s, dst_ref=r, send_sem=ss, recv_sem=rr, device_id=p, device_id_type=MESH
        )

    def arrived(ref, sem):
        pltpu.make_async_copy(ref, ref, sem).wait()

    pair_copy = remote(
        wp.at[pl.ds(pl.multiple_of((1 - c) * half, half), half)], pairb, pair_s, pair_r, partner
    )
    pair_copy.start()
    pair_copy.wait_recv()
    mine = wp[pl.ds(pl.multiple_of(c * half, half), half)]
    W[z, c, q, p] = mine + pairb[...]

    def unit(s):
        return (z + jnp.where(s % 2 == 1, (s + 1) // 2, NZ - s // 2)) % NZ

    def piece(s, i):
        return W.at[unit(s), c, q, (p + i + 4) % 4]

    def row(s, j):
        return W.at[unit(s), c, (q + j + 4) % 4]

    def p1_copy(s, v):
        return remote(piece(s, 0), piece(s, 0), p1_s.at[s, v], p1_r.at[s, v], first[v])

    def p1h_copy(s, v):
        w = piece(s, 2 * v - 1).at[pl.ds(v * quarter, quarter)]
        return remote(w, w, p1h_s.at[s, v], p1h_r.at[s, v], first[v])

    def p2_copy(s, v):
        return remote(row(s, 0), row(s, 0), p2_s.at[s, v], p2_r.at[s, v], second[v])

    def p2h_copy(s, v):
        w = row(s, 2 * v - 1).at[pl.ds(2 * v, 2)]
        return remote(w, w, p2h_s.at[s, v], p2h_r.at[s, v], second[v])

    def hand_copy(s, j):
        return remote(row(s, j), row(s, j), h_s.at[s, j + 1], h_r.at[s], partner)

    one = W.at[0, 0, 0, 0]
    one_part = one.at[pl.ds(0, quarter)]
    one_row = W.at[0, 0, 0]
    two = W.at[0, 0, 0, pl.ds(0, 2)]
    whole_half = W.at[0, 0]

    def z_pass(s, to, up):
        return remote(piece(s, 0), piece(s, 0), z_s.at[to], z_r.at[to], above if up else below)

    def stage1(s):
        for v in range(2):
            p1_copy(s, v).start()

    def z_step(s):
        arrived(one, z_r.at[s])
        stage1(s)

        @pl.when((s % 2 == 1) & (s + 2 < NC))
        def _():
            z_pass(s, s + 2, False).start()

        @pl.when((s % 2 == 0) & (s + 2 < NC))
        def _():
            z_pass(s, s + 2, True).start()

    def stage2(s):
        for v in range(2):
            arrived(one, p1_r.at[s, v])
            p1h_copy(s, v).start()

    def stage3(s):
        for v in range(2):
            arrived(one_part, p1h_r.at[s, v])
        for v in range(2):
            p2_copy(s, v).start()
        hand_copy(s, 0).start()

    def stage4(s):
        for v in range(2):
            arrived(one_row, p2_r.at[s, v])
            p2h_copy(s, v).start()
            hand_copy(s, 2 * v - 1).start()

    def stage5(s):
        for v in range(2):
            arrived(two, p2h_r.at[s, v])
        hand_copy(s, 2).start()

    length = tab[T_LEN]

    def row_scales(lo, hi):
        @pl.loop(lo, hi)
        def _(b):
            x_copy(b).wait()
            r0 = pl.multiple_of(b * BLK, BLK)
            rows_b = pl.ds(r0, BLK)
            total = jnp.zeros((BLK, HD), F32)
            for k in range(depth // HD):
                v = xv[rows_b, k * HD:(k + 1) * HD].astype(F32)
                total = total + v * v
            mean = jnp.sum(total, axis=1, keepdims=True) * (1.0 / depth)
            scale = jnp.broadcast_to(lax.rsqrt(mean + EPS), (BLK, HD))
            p = r0 + lax.broadcasted_iota(I32, (BLK, HD), 0)
            rs[rows_b, :] = jnp.where(p < length, scale, 0.0)

    stage1(0)
    z_pass(0, 1, False).start()
    z_pass(0, 2, True).start()
    row_scales(0, 2)
    stage2(0)
    z_step(1)
    row_scales(2, 4)
    stage3(0)
    stage2(1)
    z_step(2)
    row_scales(4, 6)
    stage4(0)
    stage3(1)
    stage2(2)
    row_scales(6, NB)
    stage5(0)
    z_step(3)
    cs_copy.wait()
    for j in range(NC):
        fin[j * NS + ZERO] = jnp.zeros((BLK, CW), BF)

    def compute(j):
        n = unit(j)
        tile = 3 * BLK

        @pl.loop(0, NB // 3)
        def _(i):
            r0 = pl.multiple_of(i * tile, tile)
            rows_i = pl.ds(r0, tile)
            w = [W[n, 0, gg // 4, gg % 4] if cc == 0 else W[n, 1, gg % 4, gg // 4]
                 for gg in range(16) for cc in range(2)]
            a = jnp.dot(xv[rows_i, :], jnp.concatenate(w, axis=0), preferred_element_type=F32)
            acc[...] = a * rs[rows_i, :]

            @pl.when(n < NC // 2)
            def _():
                k = acc[...]
                s = lax.rsqrt(jnp.mean(k * k, axis=1, keepdims=True) + EPS)
                k = k * s * kg[...]
                turned = k * csv[0, rows_i, :] + pltpu.roll(k, HD // 2, 1) * csv[1, rows_i, :]
                own[pl.ds(3 * i, 3)] = turned.astype(BF).reshape(3, BLK, HD)

            @pl.when(n >= NC // 2)
            def _():
                own[pl.ds(3 * i, 3)] = acc[...].astype(BF).reshape(3, BLK, CW)

    def pair_block_copy(j):
        return remote(stp.at[j], prv.at[j], a2a_s.at[j, 0], a2a_r.at[j, 0], partner)

    def hop_a(j, h):
        s = sta.at[j] if h == 0 else ra[h - 1].at[j, pl.ds(0, CA[h])]
        return remote(s, ra[h].at[j], a2a_s.at[j, 1 + h], a2a_r.at[j, 1 + h], far)

    def hop_b(j, h):
        s = stb.at[j] if h == 0 else rb[h - 1].at[j, pl.ds(0, CB[h])]
        return remote(s, rb[h].at[j], a2a_s.at[j, 5 + h], a2a_r.at[j, 5 + h], near)

    def send_pair(j):
        for e in range(5):
            stp[j, e] = own[tab[T_P + e]]
        pair_block_copy(j).start()
        for e in range(5):
            fin[j * NS + e] = own[tab[T_O + e]]

    def send_first(j):
        base = j * NS
        pair_block_copy(j).wait_recv()
        for e in range(5):
            fin[base + 5 + e] = prv[j, e]
        for e in range(CA[0]):
            sta[j, e] = fin[base + tab[T_A + e]]
        hop_a(j, 0).start()
        for e in range(CB[0]):
            stb[j, e] = fin[base + tab[T_B + e]]
        hop_b(j, 0).start()

    def forward(j, h):
        hop_a(j, h - 1).wait_recv()
        if h < 4:
            hop_a(j, h).start()
        if h < 4:
            hop_b(j, h - 1).wait_recv()
        if h < 3:
            hop_b(j, h).start()
        base = j * NS
        for q in range(CA[h - 1]):
            fin[base + BASE_A[h - 1] + q] = ra[h - 1][j, q]
        if h < 4:
            for q in range(CB[h - 1]):
                fin[base + BASE_B[h - 1] + q] = rb[h - 1][j, q]

    def step_in_range(stage, s):
        @pl.when(s < NC)
        def _():
            stage(s)

    @pl.loop(0, NC + 4)
    def _(j):
        @pl.when(j < NC)
        def _():
            arrived(whole_half, h_r.at[j])
            compute(j)
            send_pair(j)

            @pl.when(j == 0)
            def _():
                stage4(1)
                stage3(2)

            @pl.when((j > 0) & (j + 2 < NC))
            def _():
                stage4(j + 2)

            step_in_range(stage2, j + 3)
            send_first(j)
            step_in_range(z_step, j + 4)

            @pl.when(j == 0)
            def _():
                stage5(1)
                stage4(2)

            @pl.when(j == 1)
            def _():
                stage5(2)

        for h in (1, 2, 3, 4):
            @pl.when((j - h >= 0) & (j - h < NC))
            def _():
                forward(j - h, h)

        step_in_range(stage3, j + 3)

        @pl.when((j > 0) & (j + 2 < NC))
        def _():
            stage5(j + 2)

    for page in range(PAGES):
        slot, chip = tab[T_F + page], tab[T_J + page]
        for n in range(NC):
            o = (n + NZ - chip) % NZ
            s = jnp.where(o == 0, 0, jnp.where(o <= NZ // 2, 2 * o - 1, 2 * (NZ - o)))
            out[page, :, n * CW:(n + 1) * CW] = fin[s * NS + slot]

    pair_copy.wait_send()
    for k in range(1, NC):
        arrived(one, z_s.at[k])

    @pl.loop(0, NC)
    def _(s):
        for v in range(2):
            p1_copy(s, v).wait_send()
            p1h_copy(s, v).wait_send()
            p2_copy(s, v).wait_send()
            p2h_copy(s, v).wait_send()
        for j in (-1, 0, 1, 2):
            hand_copy(s, j).wait_send()
        pair_block_copy(s).wait_send()
        for h in range(4):
            hop_a(s, h).wait_send()
        for h in range(3):
            hop_b(s, h).wait_send()


def rotary(rows):
    m = np.arange(HD // 2, dtype=np.float64)
    angle = np.arange(rows, dtype=np.float64)[:, None] * (1000000.0 ** (-2.0 * m / HD))[None, :]
    cos, sin = np.cos(angle), np.sin(angle)
    return np.stack([np.concatenate([cos, cos], 1), np.concatenate([-sin, sin], 1)]).astype(np.float32)


def local(hidden, lengths, kv_weight, input_gain, key_gain):
    rows, depth = hidden.shape
    piece = depth // 16
    vm, sm, anym = (pl.BlockSpec(memory_space=s) for s in (pltpu.VMEM, pltpu.SMEM, pl.ANY))
    tab = pl.pallas_call(
        table_kernel,
        out_shape=jax.ShapeDtypeStruct((T_SIZE,), I32),
        in_specs=[sm],
        out_specs=sm,
        scratch_shapes=[pltpu.SMEM((2 * NZ + 1,), I32)],
        name="tables",
    )(lengths)
    blk = lambda *s: pltpu.VMEM((*s, BLK, CW), BF)
    dma = lambda *s: pltpu.SemaphoreType.DMA(s)
    half = piece // 2
    pages = pl.pallas_call(
        functools.partial(main_kernel, rows, depth),
        out_shape=jax.ShapeDtypeStruct((PAGES, BLK, NC * CW), BF),
        in_specs=[sm, vm, vm, vm, anym, anym],
        out_specs=vm,
        scratch_shapes=[
            pltpu.VMEM((rows, depth), BF),
            pltpu.VMEM((2, rows, HD), F32),
            pltpu.VMEM((rows, HD), F32),
            pltpu.VMEM((NZ, 2, 4, 4, half, HD), BF),
            pltpu.VMEM((HD, piece + HD // 2), F32),
            pltpu.VMEM((piece, HD), BF),
            pltpu.VMEM((half, HD), BF),
            blk(NB),
            pltpu.VMEM((3 * BLK, CW), F32),
            blk(NC * NS),
            blk(NC, 5),
            blk(NC, 5),
            blk(NC, CA[0]),
            blk(NC, CB[0]),
            *[blk(NC, s) for s in CA],
            *[blk(NC, s) for s in CB],
            dma(NB),
            *[pltpu.SemaphoreType.DMA] * 3,
            dma(NC),
            dma(NC),
            *[dma(NC, 2)] * 8,
            dma(NC, 4),
            dma(NC),
            dma(NC, 8),
            dma(NC, 8),
        ],
        compiler_params=pltpu.CompilerParams(
            collective_id=0, has_side_effects=True, vmem_limit_bytes=66_000_000
        ),
        name="recompute",
    )(tab, kv_weight.T, input_gain[None, :], key_gain[None, :], jnp.asarray(rotary(rows)), hidden)
    live = tab[T_F:T_F + PAGES] != ZERO
    return jnp.where(live[:, None, None], pages, jnp.zeros((), BF))


def solution(mesh):
    placed = (P(("grp", "tp"), None), P("grp", None), P("grp", "tp"), P(), P())
    return jax.shard_map(
        local,
        mesh=mesh,
        in_specs=placed,
        out_specs=P(("grp", "tp"), None, None),
        check_vma=False,
    )
```
